256 devices in a mesh: light: 4 (over x), view: 64 (over y, z, core).
Axes of the slice: x: 4, y: 4, z: 8, core: 2. Of those that a mesh axis runs over, the one named last changes fastest.
Arguments:
- density: float32 [512, 256, 4096], P('view', 'light'), may hold values from 0 to 1
- tables: float32 [8, 4, 16], replicated, may hold values from 0.2 to 2
- table_index: int32 [4, 64], P('light', 'view'), may hold values from 0 to 7
- light_code: int32 [4], replicated, may hold values from -1 to 1, as said below
- light_tint: float32 [4, 3], replicated, may hold values from 0.25 to 1
Outputs:
- image: float32 [4, 256, 4096], P(None, ('light', 'view'))
The draws below stay inside these ranges and needn't reach their ends.
Inputs may be any that keep to these rules, and one draw needn't show every extreme that they name: `light_code`: each of -1, 0 and 1 occurs.
All inputs are finite; a program needn't handle non-finite values.
Results may differ from the reference program's by a relative error of at most 0.0003.
Values sent between devices are 32-bit elements; how exact they have to be, the bound alone decides.
A program may use at most 256 MiB of HBM per device.

```python
import math
import jax
import jax.numpy as jnp
from jax import lax

A_DEV = 64
B_DEV = 8
COLS = 4096
LIGHTS = 4
TABLES = 8
KNOTS = 16
NA = 256
NB = 512
N_LIGHT = 4
N_VIEW = 64


def draw_light_code(key, part):
    extra = jax.random.randint(jax.random.fold_in(key, 7), (LIGHTS - 3,), -1, 2, dtype=jnp.int32)
    base = jnp.concatenate([jnp.array([-1, 0, 1], dtype=jnp.int32), extra])
    return jax.random.permutation(jax.random.fold_in(key, 11), base)


def touch_ends(drawn, stream_key, least, largest):
    extent = drawn.shape
    index_at = [jax.random.randint(jax.random.fold_in(stream_key, axis), (), 0, extent[axis]) for axis in range(len(extent))]
    drawn = drawn.at[tuple(index_at)].set(least)
    longest = extent.index(max(extent))
    index_at[longest] = (index_at[longest] + 1) % extent[longest]
    return drawn.at[tuple(index_at)].set(largest)


def block_levels(key, extent, pieces, least, largest):
    gain, own = 1.0, jax.random.fold_in(key, 6)
    for position, parts in pieces:
        draws = jnp.exp(jax.random.uniform(jax.random.fold_in(own, position), (parts,), jnp.float32, least / len(pieces), largest / len(pieces)))
        gain = gain * jnp.repeat(draws, extent[position] // parts).reshape([-1 if axis == position else 1 for axis in range(len(extent))])
    return gain


def setup_inputs(seed: int = 0) -> dict:
    splits = jax.random.split(jax.random.key(seed), 6)
    density = jnp.clip(1.0 * jax.random.uniform(splits[0], (NB, NA, COLS), jnp.float32) ** block_levels(splits[0], (NB, NA, COLS), ((0, 64), (1, 4)), -0.2, 0.2), 0.0, 1.0)
    tables = jnp.clip(jax.random.uniform(splits[1], (TABLES, 4, KNOTS), jnp.float32, 0.2, 2.0), 0.2, 2.0)
    table_index = touch_ends(jax.random.randint(splits[2], (N_LIGHT, N_VIEW), 0, TABLES), jax.random.fold_in(splits[2], 1), 0, TABLES - 1).astype(jnp.int32)
    light_code = draw_light_code(jax.random.fold_in(splits[5], 71), 0)
    light_tint = jnp.clip(jnp.exp(jax.random.uniform(splits[4], (LIGHTS, 3), jnp.float32, math.log(0.25), math.log(1.0))), 0.25, 1.0)
    return dict(density=density, tables=tables, table_index=table_index, light_code=light_code, light_tint=light_tint)


blur_side = 0.25


def table_values(field, table):
    knot_count = table.shape[1]
    scaled = field * (knot_count - 1)
    floor_at = jnp.clip(jnp.floor(scaled), 0.0, knot_count - 2.0)
    fraction = scaled - floor_at
    shape_tail = (1,) * field.ndim
    result = jnp.zeros((table.shape[0],) + field.shape, jnp.float32)
    for knot_at in range(knot_count - 1):
        left_value = table[:, knot_at].reshape((-1,) + shape_tail)
        right_value = table[:, knot_at + 1].reshape((-1,) + shape_tail)
        value_here = left_value * (1.0 - fraction[None]) + right_value * fraction[None]
        result = jnp.where((floor_at == knot_at)[None], value_here, result)
    return result


def cone_blur(fronts, codes):
    width = fronts.shape[-1]
    padded = jnp.pad(fronts, ((0, 0), (0, 0), (2, 2)))
    offsets = jnp.arange(-2, 3, dtype=jnp.int32)
    code_col = codes[:, None]
    basis = jnp.where(offsets[None] == code_col, 1.0 - 2.0 * blur_side, 0.0) + jnp.where(jnp.abs(offsets[None] - code_col) == 1, blur_side, 0.0)
    total = jnp.zeros_like(fronts)
    for shift_idx in range(5):
        shift_by = shift_idx - 2
        moved = padded[:, :, 2 - shift_by:2 - shift_by + width]
        total = total + basis[:, shift_idx][:, None, None] * moved
    return total


def reference(density, tables, table_index, light_code, light_tint):
    volume = density.reshape(N_VIEW, B_DEV, NA, COLS)

    def brick(carry, inputs):
        rgb_acc, clear_acc = carry
        slab, row_tables = inputs
        front = jnp.ones((LIGHTS, B_DEV, COLS), jnp.float32)
        rgb_parts = []
        clear_parts = []
        for light_brick in range(N_LIGHT):
            cells = slab[:, light_brick * A_DEV:(light_brick + 1) * A_DEV]
            props = table_values(cells, tables[row_tables[light_brick]])
            sigma = props[0]
            color = props[1:]
            optical = sigma / NA
            before = jnp.cumsum(optical, axis=1) - optical
            shadow = jnp.exp(-before)
            lighting = jnp.einsum('lk,lbc->kbc', light_tint, front, precision=lax.Precision.HIGHEST)
            view_depth = sigma / NB
            view_before = jnp.cumsum(view_depth, axis=0) - view_depth
            weight = jnp.exp(-view_before) * (1.0 - jnp.exp(-view_depth)) * shadow
            rgb_parts.append(jnp.sum(weight[None] * color * lighting[:, :, None, :], axis=1))
            clear_parts.append(jnp.exp(-jnp.sum(view_depth, axis=0)))
            front = cone_blur(front * jnp.exp(-jnp.sum(optical, axis=1))[None], light_code)
        rgb_brick = jnp.concatenate(rgb_parts, axis=1)
        clear_brick = jnp.concatenate(clear_parts, axis=0)
        rgb_acc = rgb_acc + clear_acc[None] * rgb_brick
        clear_acc = clear_acc * clear_brick
        return (rgb_acc, clear_acc), None

    start = (jnp.zeros((3, NA, COLS), jnp.float32), jnp.ones((NA, COLS), jnp.float32))
    (rgb_acc, clear_acc), unused = lax.scan(brick, start, (volume, table_index.T))
    return jnp.concatenate([rgb_acc, clear_acc[None]], axis=0)
```

```python
import functools
import math

import jax
import jax.numpy as jnp
from jax import lax
from jax.experimental import pallas as pl
from jax.experimental.pallas import tpu as pltpu
from jax.sharding import PartitionSpec as P

MESH = pl.DeviceIdType.MESH
LANES = 128
SUB = 8
NZ, NCORE = 8, 2


def lookup(row, index):
    return jnp.take_along_axis(row, index, axis=1, mode="promise_in_bounds")


def over(front, back):
    out = [front[k] + front[3] * back[k] for k in range(3)]
    return out + [front[3] * back[3]]


def kernel(
    nx, ny, layers, slices, columns, knots, table_count, lights,
    index_ref, code_ref, tint_ref, tables_ref, density_ref, out_ref,
    dens, keep, tab, leave, leave_in, fronts, light, part, core_in, z_in, y_part, y_in,
    dens_sem, leave_send, leave_recv, core_send, core_recv, z_send, z_recv, y_send, y_recv,
):
    x = lax.axis_index("light")
    v = lax.axis_index("view")
    core = v % NCORE
    z = (v // NCORE) % NZ
    y = v // (NCORE * NZ)
    blocks = columns // (SUB * LANES)
    tiles_a = slices // SUB
    tiles = columns // LANES

    def at_view(yy, zz, cc):
        return {"view": (yy * NZ + zz) * NCORE + cc}

    for block in range(blocks):
        pltpu.make_async_copy(
            density_ref.at[:, :, pl.ds(block * SUB * SUB, SUB * SUB)], dens.at[block], dens_sem.at[block]
        ).start()

    barrier = pltpu.get_barrier_semaphore()
    peers = [at_view(y, z, 1 - core)]
    peers += [at_view(y, (z + d) % NZ, core) for d in range(1, NZ)]
    peers += [at_view((y + d) % ny, z, core) for d in range(1, ny)]
    peers += [{"light": (x + d) % nx} for d in range(1, nx)]
    for peer in peers:
        pl.semaphore_signal(barrier, inc=1, device_id=peer, device_id_type=MESH)

    chosen = tables_ref[index_ref[0, 0]]
    tab[...] = jnp.zeros_like(tab)
    tab[0:4, 0:knots] = chosen
    knot_values = tab[...]
    lane = lax.broadcasted_iota(jnp.int32, (SUB, LANES), 1)
    rise = jnp.where(lane < knots - 1, pltpu.roll(knot_values, LANES - 1, 1) - knot_values, 0.0)
    base = knot_values - rise * lane.astype(jnp.float32)
    slope = rise * float(knots - 1)
    depth_scale = -math.log2(math.e) * math.exp2(-9)
    rows = []
    for q in range(4):
        scale = depth_scale if q == 0 else 1.0
        rows.append(
            tuple(jnp.broadcast_to(t[q : q + 1] * scale, (SUB, LANES)) for t in (base, slope))
        )

    def cell_index(d):
        return (d * float(knots - 1)).astype(jnp.int32)

    for block in range(blocks):
        pltpu.make_async_copy(dens.at[block], dens.at[block], dens_sem.at[block]).wait()

        def first(tile, sums, block=block):
            sums = list(sums)
            for row in range(SUB):
                for b in range(layers):
                    d = dens[block, b, tile, pl.ds(row, SUB, stride=SUB), :]
                    k = cell_index(d)
                    depth = lookup(rows[0][0], k) + lookup(rows[0][1], k) * d
                    keep[block, tile * SUB + row, b] = jnp.exp2(depth)
                    sums[b] = sums[b] + depth
            return tuple(sums)

        zero = jnp.zeros((SUB, LANES), jnp.float32)
        sums = lax.fori_loop(0, tiles_a, first, (zero,) * layers)
        for b in range(layers):
            leave[block, pl.ds(b * SUB, SUB)] = jnp.exp2(sums[b] * 2.0)
        if block == 0:
            pl.semaphore_wait(barrier, len(peers))
        for d in range(1, nx):

            @pl.when(x + d < nx)
            def _(d=d, block=block):
                pltpu.make_async_remote_copy(
                    src_ref=leave.at[block], dst_ref=leave_in.at[x, block],
                    send_sem=leave_send.at[d, block], recv_sem=leave_recv.at[x, block],
                    device_id={"light": (x + d) % nx}, device_id_type=MESH,
                ).start()

    column = lax.broadcasted_iota(jnp.int32, (layers, columns), 1)
    fronts[...] = jnp.ones_like(fronts)

    def moved(values, by):
        rolled = pltpu.roll(values, by % columns, 1)
        inside = column >= by if by > 0 else column < columns + by
        return jnp.where(inside, rolled, 0.0)

    for stage in range(nx - 1):

        @pl.when(x > stage)
        def _(stage=stage):
            for block in range(blocks):
                pltpu.make_async_copy(
                    leave_in.at[stage, block], leave_in.at[stage, block], leave_recv.at[stage, block]
                ).wait()
            gone = jnp.concatenate(
                [leave_in[stage, t // SUB, pl.ds(t % SUB, layers, stride=SUB), :] for t in range(tiles)], axis=1
            )
            for drift in (-1, 0, 1):
                value = fronts[drift + 1] * gone
                total = 0.0
                for offset, share in ((drift - 1, 0.25), (drift, 0.5), (drift + 1, 0.25)):
                    total = total + share * (moved(value, offset) if offset else value)
                fronts[drift + 1] = total

    for k in range(3):
        tint = [0.0, 0.0, 0.0]
        for l in range(lights):
            for drift in (-1, 0, 1):
                tint[drift + 1] = tint[drift + 1] + jnp.where(code_ref[l] == drift, tint_ref[l, k], 0.0)
        for t in range(tiles):
            cols = pl.ds(t * LANES, LANES)
            light[k, t // SUB, pl.ds(t % SUB, layers, stride=SUB), :] = (
                fronts[0, :, cols] * tint[0] + fronts[1, :, cols] * tint[1] + fronts[2, :, cols] * tint[2]
            )

    def core_copy(block):
        return pltpu.make_async_remote_copy(
            src_ref=part.at[block, 1 - core], dst_ref=core_in.at[block],
            send_sem=core_send.at[block], recv_sem=core_recv.at[block],
            device_id=at_view(y, z, 1 - core), device_id_type=MESH,
        )

    def z_copy(block, d):
        to = (z + d) % NZ
        return pltpu.make_async_remote_copy(
            src_ref=part.at[block, core, to], dst_ref=z_in.at[block, z],
            send_sem=z_send.at[block, d], recv_sem=z_recv.at[block, z],
            device_id=at_view(y, to, core), device_id_type=MESH,
        )

    def y_copy(block, d):
        to = (y + d) % ny
        return pltpu.make_async_remote_copy(
            src_ref=y_part.at[block, to], dst_ref=y_in.at[block, y],
            send_sem=y_send.at[block, d], recv_sem=y_recv.at[block, y],
            device_id=at_view(to, z, core), device_id_type=MESH,
        )

    z_order = (4, 1, 7, 2, 6, 3, 5)

    def join_cores(block):
        core_copy(block).wait_recv()

        def join(zz):
            for yy in range(ny):
                mine = [part[block, core, zz, yy, k] for k in range(4)]
                other = [core_in[block, zz, yy, k] for k in range(4)]
                front = [jnp.where(core == 0, m, o) for m, o in zip(mine, other)]
                back = [jnp.where(core == 0, o, m) for m, o in zip(mine, other)]
                joined = over(front, back)
                for k in range(4):
                    part[block, core, zz, yy, k] = joined[k]

        @pl.loop(0, NZ)
        def _(zz):
            join(zz)

        for d in z_order:
            z_copy(block, d).start()
        for yy in range(ny):
            for k in range(4):
                z_in[block, z, yy, k] = part[block, core, z, yy, k]

    for block in range(blocks):

        def second(tile, shadow, block=block):
            shadow = list(shadow)
            for row in range(SUB):
                clear = None
                total = [None] * 3
                for b in range(layers):
                    d = dens[block, b, tile, pl.ds(row, SUB, stride=SUB), :]
                    k = cell_index(d)
                    stays = keep[block, tile * SUB + row, b]
                    if clear is None:
                        weight = (1.0 - stays) * shadow[b]
                        clear = stays
                    else:
                        after = clear * stays
                        weight = (clear - after) * shadow[b]
                        clear = after
                    shadow[b] = shadow[b] * (stays * stays)
                    for c in range(3):
                        color = lookup(rows[c + 1][0], k) + lookup(rows[c + 1][1], k) * d
                        term = color * (weight * light[c, block, pl.ds(b * SUB, SUB), :])
                        total[c] = term if total[c] is None else total[c] + term
                zz = (tile % 2) * (SUB // NCORE) + row // NCORE
                for c in range(3):
                    part[block, row % NCORE, zz, tile // 2, c] = total[c]
                part[block, row % NCORE, zz, tile // 2, 3] = clear
            return tuple(shadow)

        one = jnp.ones((SUB, LANES), jnp.float32)
        lax.fori_loop(0, tiles_a, second, (one,) * layers)
        core_copy(block).start()
        if block:
            join_cores(block - 1)
    join_cores(blocks - 1)

    for block in range(blocks):
        for i in range(1, NZ):
            zz = (z + i) % NZ
            pltpu.make_async_copy(z_in.at[block, zz], z_in.at[block, zz], z_recv.at[block, zz]).wait()

        @pl.loop(0, ny)
        def _(yy):
            total = [z_in[block, 0, yy, k] for k in range(4)]
            for i in range(1, NZ):
                total = over(total, [z_in[block, i, yy, k] for k in range(4)])
            for k in range(4):
                y_part[block, yy, k] = total[k]

        for d in range(1, ny):
            y_copy(block, d).start()
        for k in range(4):
            y_in[block, y, k] = y_part[block, y, k]

    for block in range(blocks):
        for i in range(1, ny):
            yy = (y + i) % ny
            pltpu.make_async_copy(y_in.at[block, yy], y_in.at[block, yy], y_recv.at[block, yy]).wait()
        total = [y_in[block, 0, k] for k in range(4)]
        for i in range(1, ny):
            total = over(total, [y_in[block, i, k] for k in range(4)])
        for k in range(4):
            out_ref[k, pl.ds(block * SUB, SUB)] = total[k]

    for block in range(blocks):
        for d in range(1, nx):

            @pl.when(x + d < nx)
            def _(d=d, block=block):
                pltpu.make_async_copy(leave.at[block], leave.at[block], leave_send.at[d, block]).wait()

        core_copy(block).wait_send()
        for d in range(1, NZ):
            z_copy(block, d).wait_send()
        for d in range(1, ny):
            y_copy(block, d).wait_send()


def local(density, tables, table_index, light_code, light_tint):
    layers, slices, columns = density.shape
    nx, ny = lax.axis_size("light"), lax.axis_size("view") // (NZ * NCORE)
    table_count, _, knots = tables.shape
    tiles = columns // LANES
    blocks = tiles // SUB
    tiled = density.reshape(layers, slices // SUB, SUB, tiles, LANES).transpose(0, 1, 3, 2, 4)
    tiled = tiled.reshape(layers, slices // SUB, tiles * SUB, LANES)
    f32 = jnp.float32
    image = pl.pallas_call(
        functools.partial(kernel, nx, ny, layers, slices, columns, knots, table_count, light_code.shape[0]),
        out_shape=jax.ShapeDtypeStruct((4, tiles, LANES), f32),
        in_specs=[pl.BlockSpec(memory_space=pltpu.SMEM)] * 3
        + [pl.BlockSpec(memory_space=pltpu.VMEM), pl.BlockSpec(memory_space=pl.ANY)],
        out_specs=pl.BlockSpec(memory_space=pltpu.VMEM),
        scratch_shapes=[
            pltpu.VMEM((blocks, layers, slices // SUB, SUB * SUB, LANES), f32),
            pltpu.VMEM((blocks, slices, layers, SUB, LANES), f32),
            pltpu.VMEM((SUB, LANES), f32),
            pltpu.VMEM((blocks, layers * SUB, LANES), f32),
            pltpu.VMEM((nx, blocks, layers * SUB, LANES), f32),
            pltpu.VMEM((3, layers, columns), f32),
            pltpu.VMEM((3, blocks, layers * SUB, LANES), f32),
            pltpu.VMEM((blocks, NCORE, NZ, ny, 4, SUB, LANES), f32),
            pltpu.VMEM((blocks, NZ, ny, 4, SUB, LANES), f32),
            pltpu.VMEM((blocks, NZ, ny, 4, SUB, LANES), f32),
            pltpu.VMEM((blocks, ny, 4, SUB, LANES), f32),
            pltpu.VMEM((blocks, ny, 4, SUB, LANES), f32),
            pltpu.SemaphoreType.DMA((blocks,)),
            pltpu.SemaphoreType.DMA((nx, blocks)),
            pltpu.SemaphoreType.DMA((nx, blocks)),
            pltpu.SemaphoreType.DMA((blocks,)),
            pltpu.SemaphoreType.DMA((blocks,)),
            pltpu.SemaphoreType.DMA((blocks, NZ)),
            pltpu.SemaphoreType.DMA((blocks, NZ)),
            pltpu.SemaphoreType.DMA((blocks, ny)),
            pltpu.SemaphoreType.DMA((blocks, ny)),
        ],
        compiler_params=pltpu.CompilerParams(
            collective_id=0, has_side_effects=True, vmem_limit_bytes=60 * 1024 * 1024
        ),
    )(table_index, light_code, light_tint, tables, tiled)
    return image.reshape(4, 1, columns)


def solution(mesh):
    return jax.shard_map(
        local,
        mesh=mesh,
        in_specs=(P("view", "light", None), P(), P("light", "view"), P(), P()),
        out_specs=P(None, ("light", "view"), None),
        check_vma=False,
    )
```

```python
import functools
import math

import jax
import jax.numpy as jnp
from jax import lax
from jax.experimental import pallas as pl
from jax.experimental.pallas import tpu as pltpu
from jax.sharding import PartitionSpec as P

MESH = pl.DeviceIdType.MESH
LANES = 128
SUB = 8
NZ, NCORE = 8, 2


def lookup(row, index):
    numbers = lax.GatherDimensionNumbers(
        offset_dims=(), collapsed_slice_dims=(1,), start_index_map=(1,),
        operand_batching_dims=(0,), start_indices_batching_dims=(0,),
    )
    return lax.gather(
        row, index[:, :, None], numbers, (1, 1), mode=lax.GatherScatterMode.PROMISE_IN_BOUNDS
    )


def over(front, back):
    out = [front[k] + front[3] * back[k] for k in range(3)]
    return out + [front[3] * back[3]]


def kernel(
    nx, ny, layers, slices, columns, knots, table_count, lights,
    index_ref, code_ref, tint_ref, tables_ref, density_ref, out_ref,
    dens, cells, knot, keep, tab, leave, leave_in, fronts, light, part, core_in, pair_in, z_in, y_part, y_in,
    dens_sem, leave_send, leave_recv, core_send, core_recv, pair_send, pair_recv, z_send, z_recv, y_send, y_recv,
):
    x = lax.axis_index("light")
    v = lax.axis_index("view")
    core = v % NCORE
    z = (v // NCORE) % NZ
    y = v // (NCORE * NZ)
    blocks = columns // (SUB * LANES)
    tiles_a = slices // SUB
    tiles = columns // LANES

    def at_view(yy, zz, cc):
        return {"view": (yy * NZ + zz) * NCORE + cc}

    for block in range(blocks):
        pltpu.make_async_copy(
            density_ref.at[:, :, pl.ds(block * SUB * SUB, SUB * SUB)], dens.at[block], dens_sem.at[block]
        ).start()

    barrier = pltpu.get_barrier_semaphore()
    peers = [at_view(y, z, 1 - core)]
    peers += [at_view(y, (z + d) % NZ, core) for d in range(1, NZ)]
    peers += [at_view((y + d) % ny, z, core) for d in range(1, ny)]
    peers += [{"light": (x + d) % nx} for d in range(1, nx)]
    for peer in peers:
        pl.semaphore_signal(barrier, inc=1, device_id=peer, device_id_type=MESH)

    chosen = tables_ref[index_ref[0, 0]]
    tab[...] = jnp.zeros_like(tab)
    tab[0:4, 0:knots] = chosen
    knot_values = tab[...]
    lane = lax.broadcasted_iota(jnp.int32, (SUB, LANES), 1)
    rise = jnp.where(lane < knots - 1, pltpu.roll(knot_values, LANES - 1, 1) - knot_values, 0.0)
    base = knot_values - rise * lane.astype(jnp.float32)
    slope = rise * float(knots - 1)
    depth_scale = -math.log2(math.e) * math.exp2(-9)
    rows = []
    for q in range(4):
        scale = depth_scale if q == 0 else 1.0
        rows.append(
            tuple(jnp.broadcast_to(t[q : q + 1] * scale, (SUB, LANES)) for t in (base, slope))
        )

    def cell_index(d):
        return (d * float(knots - 1)).astype(jnp.int32)

    for block in range(blocks):
        pltpu.make_async_copy(dens.at[block], dens.at[block], dens_sem.at[block]).wait()

        def first(tile, sums, block=block):
            sums = list(sums)
            for row in range(SUB):
                for b in range(layers):
                    d = dens[block, b, tile, pl.ds(row, SUB, stride=SUB), :]
                    k = cell_index(d)
                    depth = lookup(rows[0][0], k) + lookup(rows[0][1], k) * d
                    keep[block, tile * SUB + row, b] = jnp.exp2(depth)
                    cells[block, tile * SUB + row, b] = d
                    knot[block, tile * SUB + row, b] = k
                    sums[b] = sums[b] + depth
            return tuple(sums)

        zero = jnp.zeros((SUB, LANES), jnp.float32)
        sums = lax.fori_loop(0, tiles_a, first, (zero,) * layers)
        for b in range(layers):
            leave[block, pl.ds(b * SUB, SUB)] = jnp.exp2(sums[b] * 2.0)
        if block == 0:
            pl.semaphore_wait(barrier, len(peers))
        for d in range(1, nx):

            @pl.when(x + d < nx)
            def _(d=d, block=block):
                pltpu.make_async_remote_copy(
                    src_ref=leave.at[block], dst_ref=leave_in.at[x, block],
                    send_sem=leave_send.at[d, block], recv_sem=leave_recv.at[x, block],
                    device_id={"light": (x + d) % nx}, device_id_type=MESH,
                ).start()

    column = lax.broadcasted_iota(jnp.int32, (layers, columns), 1)
    fronts[...] = jnp.ones_like(fronts)

    def moved(values, by):
        rolled = pltpu.roll(values, by % columns, 1)
        inside = column >= by if by > 0 else column < columns + by
        return jnp.where(inside, rolled, 0.0)

    for stage in range(nx - 1):

        @pl.when(x > stage)
        def _(stage=stage):
            for block in range(blocks):
                pltpu.make_async_copy(
                    leave_in.at[stage, block], leave_in.at[stage, block], leave_recv.at[stage, block]
                ).wait()
            gone = jnp.concatenate(
                [leave_in[stage, t // SUB, pl.ds(t % SUB, layers, stride=SUB), :] for t in range(tiles)], axis=1
            )
            for drift in (-1, 0, 1):
                value = fronts[drift + 1] * gone
                total = 0.0
                for offset, share in ((drift - 1, 0.25), (drift, 0.5), (drift + 1, 0.25)):
                    total = total + share * (moved(value, offset) if offset else value)
                fronts[drift + 1] = total

    for k in range(3):
        tint = [0.0, 0.0, 0.0]
        for l in range(lights):
            for drift in (-1, 0, 1):
                tint[drift + 1] = tint[drift + 1] + jnp.where(code_ref[l] == drift, tint_ref[l, k], 0.0)
        for t in range(tiles):
            cols = pl.ds(t * LANES, LANES)
            light[k, t // SUB, pl.ds(t % SUB, layers, stride=SUB), :] = (
                fronts[0, :, cols] * tint[0] + fronts[1, :, cols] * tint[1] + fronts[2, :, cols] * tint[2]
            )

    def core_copy(block):
        return pltpu.make_async_remote_copy(
            src_ref=part.at[block, 1 - core], dst_ref=core_in.at[block],
            send_sem=core_send.at[block], recv_sem=core_recv.at[block],
            device_id=at_view(y, z, 1 - core), device_id_type=MESH,
        )

    pair = z // 2
    odd = z % 2
    side = 2 * odd - 1
    half = NZ // 2

    def owner(j):
        return (z + side * j + NZ) % NZ

    def pair_copy(block, j):
        return pltpu.make_async_remote_copy(
            src_ref=part.at[block, core, owner(-1 - j)], dst_ref=pair_in.at[block, j],
            send_sem=pair_send.at[block, j], recv_sem=pair_recv.at[block, j],
            device_id=at_view(y, owner(-1), core), device_id_type=MESH,
        )

    def z_copy(block, j):
        return pltpu.make_async_remote_copy(
            src_ref=part.at[block, core, owner(j)], dst_ref=z_in.at[block, pair],
            send_sem=z_send.at[block, j], recv_sem=z_recv.at[block, pair],
            device_id=at_view(y, owner(j), core), device_id_type=MESH,
        )

    def y_copy(block, d):
        to = (y + d) % ny
        return pltpu.make_async_remote_copy(
            src_ref=y_part.at[block, to], dst_ref=y_in.at[block, y],
            send_sem=y_send.at[block, d], recv_sem=y_recv.at[block, y],
            device_id=at_view(to, z, core), device_id_type=MESH,
        )

    def ordered(later, mine, other):
        front = [jnp.where(later, o, m) for m, o in zip(mine, other)]
        back = [jnp.where(later, m, o) for m, o in zip(mine, other)]
        return over(front, back)

    def join_cores(block):
        core_copy(block).wait_recv()

        @pl.loop(0, NZ)
        def _(zz):
            for yy in range(ny):
                mine = [part[block, core, zz, yy, k] for k in range(4)]
                other = [core_in[block, zz, yy, k] for k in range(4)]
                joined = ordered(core == 1, mine, other)
                for k in range(4):
                    part[block, core, zz, yy, k] = joined[k]

        for j in reversed(range(half)):
            pair_copy(block, j).start()

    def join_pair(block):
        for j in reversed(range(half)):
            pair_copy(block, j).wait_recv()
            at = owner(j)
            for yy in range(ny):
                mine = [part[block, core, at, yy, k] for k in range(4)]
                other = [pair_in[block, j, yy, k] for k in range(4)]
                joined = ordered(odd == 1, mine, other)
                for k in range(4):
                    if j:
                        part[block, core, at, yy, k] = joined[k]
                    else:
                        z_in[block, pair, yy, k] = joined[k]
            if j:
                z_copy(block, j).start()

    for block in range(blocks):

        def second(tile, shadow, block=block):
            shadow = list(shadow)
            for row in range(SUB):
                clear = None
                total = [None] * 3
                for b in range(layers):
                    d = cells[block, tile * SUB + row, b]
                    k = knot[block, tile * SUB + row, b]
                    stays = keep[block, tile * SUB + row, b]
                    if clear is None:
                        weight = (1.0 - stays) * shadow[b]
                        clear = stays
                    else:
                        after = clear * stays
                        weight = (clear - after) * shadow[b]
                        clear = after
                    shadow[b] = shadow[b] * (stays * stays)
                    for c in range(3):
                        color = lookup(rows[c + 1][0], k) + lookup(rows[c + 1][1], k) * d
                        term = color * (weight * light[c, block, pl.ds(b * SUB, SUB), :])
                        total[c] = term if total[c] is None else total[c] + term
                zz = (tile % 2) * (SUB // NCORE) + row // NCORE
                for c in range(3):
                    part[block, row % NCORE, zz, tile // 2, c] = total[c]
                part[block, row % NCORE, zz, tile // 2, 3] = clear
            return tuple(shadow)

        one = jnp.ones((SUB, LANES), jnp.float32)
        lax.fori_loop(0, tiles_a, second, (one,) * layers)
        core_copy(block).start()
        if block:
            join_cores(block - 1)
    join_cores(blocks - 1)

    for block in range(blocks):
        join_pair(block)

    for block in range(blocks):
        for i in range(1, half):
            q = (pair + i) % half
            pltpu.make_async_copy(z_in.at[block, q], z_in.at[block, q], z_recv.at[block, q]).wait()

        @pl.loop(0, ny)
        def _(yy):
            total = [z_in[block, 0, yy, k] for k in range(4)]
            for i in range(1, half):
                total = over(total, [z_in[block, i, yy, k] for k in range(4)])
            for k in range(4):
                y_part[block, yy, k] = total[k]

        for d in range(1, ny):
            y_copy(block, d).start()
        for k in range(4):
            y_in[block, y, k] = y_part[block, y, k]

    for block in range(blocks):
        for i in range(1, ny):
            yy = (y + i) % ny
            pltpu.make_async_copy(y_in.at[block, yy], y_in.at[block, yy], y_recv.at[block, yy]).wait()
        total = [y_in[block, 0, k] for k in range(4)]
        for i in range(1, ny):
            total = over(total, [y_in[block, i, k] for k in range(4)])
        for k in range(4):
            out_ref[k, pl.ds(block * SUB, SUB)] = total[k]

    for block in range(blocks):
        for d in range(1, nx):

            @pl.when(x + d < nx)
            def _(d=d, block=block):
                pltpu.make_async_copy(leave.at[block], leave.at[block], leave_send.at[d, block]).wait()

        core_copy(block).wait_send()
        for j in range(half):
            pair_copy(block, j).wait_send()
        for j in range(1, half):
            z_copy(block, j).wait_send()
        for d in range(1, ny):
            y_copy(block, d).wait_send()


def local(density, tables, table_index, light_code, light_tint):
    layers, slices, columns = density.shape
    nx, ny = lax.axis_size("light"), lax.axis_size("view") // (NZ * NCORE)
    table_count, _, knots = tables.shape
    tiles = columns // LANES
    blocks = tiles // SUB
    tiled = density.reshape(layers, slices // SUB, SUB, tiles, LANES).transpose(0, 1, 3, 2, 4)
    tiled = tiled.reshape(layers, slices // SUB, tiles * SUB, LANES)
    f32 = jnp.float32
    image = pl.pallas_call(
        functools.partial(kernel, nx, ny, layers, slices, columns, knots, table_count, light_code.shape[0]),
        out_shape=jax.ShapeDtypeStruct((4, tiles, LANES), f32),
        in_specs=[pl.BlockSpec(memory_space=pltpu.SMEM)] * 3
        + [pl.BlockSpec(memory_space=pltpu.VMEM), pl.BlockSpec(memory_space=pl.ANY)],
        out_specs=pl.BlockSpec(memory_space=pltpu.VMEM),
        scratch_shapes=[
            pltpu.VMEM((blocks, layers, slices // SUB, SUB * SUB, LANES), f32),
            pltpu.VMEM((blocks, slices, layers, SUB, LANES), f32),
            pltpu.VMEM((blocks, slices, layers, SUB, LANES), jnp.int32),
            pltpu.VMEM((blocks, slices, layers, SUB, LANES), f32),
            pltpu.VMEM((SUB, LANES), f32),
            pltpu.VMEM((blocks, layers * SUB, LANES), f32),
            pltpu.VMEM((nx, blocks, layers * SUB, LANES), f32),
            pltpu.VMEM((3, layers, columns), f32),
            pltpu.VMEM((3, blocks, layers * SUB, LANES), f32),
            pltpu.VMEM((blocks, NCORE, NZ, ny, 4, SUB, LANES), f32),
            pltpu.VMEM((blocks, NZ, ny, 4, SUB, LANES), f32),
            pltpu.VMEM((blocks, NZ // 2, ny, 4, SUB, LANES), f32),
            pltpu.VMEM((blocks, NZ // 2, ny, 4, SUB, LANES), f32),
            pltpu.VMEM((blocks, ny, 4, SUB, LANES), f32),
            pltpu.VMEM((blocks, ny, 4, SUB, LANES), f32),
            pltpu.SemaphoreType.DMA((blocks,)),
            pltpu.SemaphoreType.DMA((nx, blocks)),
            pltpu.SemaphoreType.DMA((nx, blocks)),
            pltpu.SemaphoreType.DMA((blocks,)),
            pltpu.SemaphoreType.DMA((blocks,)),
            pltpu.SemaphoreType.DMA((blocks, NZ // 2)),
            pltpu.SemaphoreType.DMA((blocks, NZ // 2)),
            pltpu.SemaphoreType.DMA((blocks, NZ // 2)),
            pltpu.SemaphoreType.DMA((blocks, NZ // 2)),
            pltpu.SemaphoreType.DMA((blocks, ny)),
            pltpu.SemaphoreType.DMA((blocks, ny)),
        ],
        compiler_params=pltpu.CompilerParams(
            collective_id=0, has_side_effects=True, vmem_limit_bytes=60 * 1024 * 1024
        ),
    )(table_index, light_code, light_tint, tables, tiled)
    return image.reshape(4, 1, columns)


def solution(mesh):
    return jax.shard_map(
        local,
        mesh=mesh,
        in_specs=(P("view", "light", None), P(), P("light", "view"), P(), P()),
        out_specs=P(None, ("light", "view"), None),
        check_vma=False,
    )
```

```python
import functools
import math

import jax
import jax.numpy as jnp
from jax import lax
from jax.experimental import pallas as pl
from jax.experimental.pallas import tpu as pltpu
from jax.sharding import PartitionSpec as P

MESH = pl.DeviceIdType.MESH
LANES = 128
SUB = 8
NZ, NCORE = 8, 2


def take(table, index, axis):
    numbers = lax.GatherDimensionNumbers(
        offset_dims=(), collapsed_slice_dims=(axis,), start_index_map=(axis,),
        operand_batching_dims=(1 - axis,), start_indices_batching_dims=(1 - axis,),
    )
    return lax.gather(
        table, index[:, :, None], numbers, (1, 1), mode=lax.GatherScatterMode.PROMISE_IN_BOUNDS
    )


def over(front, back):
    out = [front[k] + front[3] * back[k] for k in range(3)]
    return out + [front[3] * back[3]]


def kernel(
    nx, ny, layers, slices, columns, knots, table_count, lights,
    index_ref, code_ref, tint_ref, tables_ref, density_ref, out_ref,
    dens, cells, knot, keep, tab, leave, leave_in, fronts, light, part, core_in, pair_in, z_in, y_part, y_in,
    dens_sem, leave_send, leave_recv, core_send, core_recv, pair_send, pair_recv, z_send, z_recv, y_send, y_recv,
):
    x = lax.axis_index("light")
    v = lax.axis_index("view")
    core = v % NCORE
    z = (v // NCORE) % NZ
    y = v // (NCORE * NZ)
    blocks = columns // (SUB * LANES)
    tiles_a = slices // SUB
    tiles = columns // LANES

    def at_view(yy, zz, cc):
        return {"view": (yy * NZ + zz) * NCORE + cc}

    for block in range(blocks):
        pltpu.make_async_copy(
            density_ref.at[:, :, pl.ds(block * SUB * SUB, SUB * SUB)], dens.at[block], dens_sem.at[block]
        ).start()

    barrier = pltpu.get_barrier_semaphore()
    peers = [at_view(y, z, 1 - core)]
    peers += [at_view(y, (z + d) % NZ, core) for d in range(1, NZ)]
    peers += [at_view((y + d) % ny, z, core) for d in range(1, ny)]
    peers += [{"light": (x + d) % nx} for d in range(1, nx)]
    for peer in peers:
        pl.semaphore_signal(barrier, inc=1, device_id=peer, device_id_type=MESH)

    chosen = tables_ref[index_ref[0, 0]]
    tab[...] = jnp.zeros_like(tab)
    tab[0:4, 0:knots] = chosen
    knot_values = tab[...]
    lane = lax.broadcasted_iota(jnp.int32, (SUB, LANES), 1)
    rise = jnp.where(lane < knots - 1, pltpu.roll(knot_values, LANES - 1, 1) - knot_values, 0.0)
    base = knot_values - rise * lane.astype(jnp.float32)
    depth_scale = -math.log2(math.e) * math.exp2(-9)

    def along_lanes(table, q):
        return jnp.broadcast_to(table[q : q + 1], (SUB, LANES))

    def along_sublanes(table, q):
        sublane = lax.broadcasted_iota(jnp.int32, (SUB, LANES), 0)
        halves = []
        for first_knot in (0, SUB):
            picked = jnp.where(lane == sublane + first_knot, along_lanes(table, q), 0.0)
            halves.append(jnp.broadcast_to(jnp.sum(picked, axis=1, keepdims=True), (SUB, LANES)))
        return halves

    split = [(along_sublanes(base * s, q), along_sublanes(rise * s, q)) for q, s in ((0, depth_scale), (1, 1.0), (2, 1.0))]
    whole = along_lanes(base, 3), along_lanes(rise, 3)

    def level(q, scaled, k):
        if q == 3:
            return take(whole[0], k, 1) + take(whole[1], k, 1) * scaled
        low = k & (SUB - 1)
        parts = [jnp.where(scaled >= float(SUB), take(t[1], low, 0), take(t[0], low, 0)) for t in split[q]]
        return parts[0] + parts[1] * scaled

    for block in range(blocks):
        pltpu.make_async_copy(dens.at[block], dens.at[block], dens_sem.at[block]).wait()

        def first(tile, sums, block=block):
            sums = list(sums)
            for row in range(SUB):
                for b in range(layers):
                    scaled = dens[block, b, tile, pl.ds(row, SUB, stride=SUB), :] * float(knots - 1)
                    k = scaled.astype(jnp.int32)
                    depth = level(0, scaled, k)
                    keep[block, tile * SUB + row, b] = jnp.exp2(depth)
                    cells[block, tile * SUB + row, b] = scaled
                    knot[block, tile * SUB + row, b] = k
                    sums[b] = sums[b] + depth
            return tuple(sums)

        zero = jnp.zeros((SUB, LANES), jnp.float32)
        sums = lax.fori_loop(0, tiles_a, first, (zero,) * layers)
        for b in range(layers):
            leave[block, pl.ds(b * SUB, SUB)] = jnp.exp2(sums[b] * 2.0)
        if block == 0:
            pl.semaphore_wait(barrier, len(peers))
        for d in range(1, nx):

            @pl.when(x + d < nx)
            def _(d=d, block=block):
                pltpu.make_async_remote_copy(
                    src_ref=leave.at[block], dst_ref=leave_in.at[x, block],
                    send_sem=leave_send.at[d, block], recv_sem=leave_recv.at[x, block],
                    device_id={"light": (x + d) % nx}, device_id_type=MESH,
                ).start()

    column = lax.broadcasted_iota(jnp.int32, (layers, columns), 1)
    fronts[...] = jnp.ones_like(fronts)

    def moved(values, by):
        rolled = pltpu.roll(values, by % columns, 1)
        inside = column >= by if by > 0 else column < columns + by
        return jnp.where(inside, rolled, 0.0)

    for stage in range(nx - 1):

        @pl.when(x > stage)
        def _(stage=stage):
            for block in range(blocks):
                pltpu.make_async_copy(
                    leave_in.at[stage, block], leave_in.at[stage, block], leave_recv.at[stage, block]
                ).wait()
            gone = jnp.concatenate(
                [leave_in[stage, t // SUB, pl.ds(t % SUB, layers, stride=SUB), :] for t in range(tiles)], axis=1
            )
            for drift in (-1, 0, 1):
                value = fronts[drift + 1] * gone
                total = 0.0
                for offset, share in ((drift - 1, 0.25), (drift, 0.5), (drift + 1, 0.25)):
                    total = total + share * (moved(value, offset) if offset else value)
                fronts[drift + 1] = total

    for k in range(3):
        tint = [0.0, 0.0, 0.0]
        for l in range(lights):
            for drift in (-1, 0, 1):
                tint[drift + 1] = tint[drift + 1] + jnp.where(code_ref[l] == drift, tint_ref[l, k], 0.0)
        for t in range(tiles):
            cols = pl.ds(t * LANES, LANES)
            light[k, t // SUB, pl.ds(t % SUB, layers, stride=SUB), :] = (
                fronts[0, :, cols] * tint[0] + fronts[1, :, cols] * tint[1] + fronts[2, :, cols] * tint[2]
            )

    def core_copy(block):
        return pltpu.make_async_remote_copy(
            src_ref=part.at[block, 1 - core], dst_ref=core_in.at[block],
            send_sem=core_send.at[block], recv_sem=core_recv.at[block],
            device_id=at_view(y, z, 1 - core), device_id_type=MESH,
        )

    pair = z // 2
    odd = z % 2
    side = 2 * odd - 1
    half = NZ // 2

    def owner(j):
        return (z + side * j + NZ) % NZ

    def pair_copy(block, j):
        return pltpu.make_async_remote_copy(
            src_ref=part.at[block, core, owner(-1 - j)], dst_ref=pair_in.at[block, j],
            send_sem=pair_send.at[block, j], recv_sem=pair_recv.at[block, j],
            device_id=at_view(y, owner(-1), core), device_id_type=MESH,
        )

    def z_copy(block, j):
        return pltpu.make_async_remote_copy(
            src_ref=part.at[block, core, owner(j)], dst_ref=z_in.at[block, pair],
            send_sem=z_send.at[block, j], recv_sem=z_recv.at[block, pair],
            device_id=at_view(y, owner(j), core), device_id_type=MESH,
        )

    def y_copy(block, d):
        to = (y + d) % ny
        return pltpu.make_async_remote_copy(
            src_ref=y_part.at[block, to], dst_ref=y_in.at[block, y],
            send_sem=y_send.at[block, d], recv_sem=y_recv.at[block, y],
            device_id=at_view(to, z, core), device_id_type=MESH,
        )

    def ordered(later, mine, other):
        front = [jnp.where(later, o, m) for m, o in zip(mine, other)]
        back = [jnp.where(later, m, o) for m, o in zip(mine, other)]
        return over(front, back)

    def join_cores(block):
        core_copy(block).wait_recv()

        @pl.loop(0, NZ)
        def _(zz):
            for yy in range(ny):
                mine = [part[block, core, zz, yy, k] for k in range(4)]
                other = [core_in[block, zz, yy, k] for k in range(4)]
                joined = ordered(core == 1, mine, other)
                for k in range(4):
                    part[block, core, zz, yy, k] = joined[k]

        for j in reversed(range(half)):
            pair_copy(block, j).start()

    def join_pair(block):
        for j in reversed(range(half)):
            pair_copy(block, j).wait_recv()
            at = owner(j)
            for yy in range(ny):
                mine = [part[block, core, at, yy, k] for k in range(4)]
                other = [pair_in[block, j, yy, k] for k in range(4)]
                joined = ordered(odd == 1, mine, other)
                for k in range(4):
                    if j:
                        part[block, core, at, yy, k] = joined[k]
                    else:
                        z_in[block, pair, yy, k] = joined[k]
            if j:
                z_copy(block, j).start()

    for block in range(blocks):

        def second(tile, shadow, block=block):
            shadow = list(shadow)
            for row in range(SUB):
                clear = None
                total = [None] * 3
                for b in range(layers):
                    scaled = cells[block, tile * SUB + row, b]
                    k = knot[block, tile * SUB + row, b]
                    stays = keep[block, tile * SUB + row, b]
                    if clear is None:
                        weight = (1.0 - stays) * shadow[b]
                        clear = stays
                    else:
                        after = clear * stays
                        weight = (clear - after) * shadow[b]
                        clear = after
                    shadow[b] = shadow[b] * (stays * stays)
                    for c in range(3):
                        color = level(c + 1, scaled, k)
                        term = color * (weight * light[c, block, pl.ds(b * SUB, SUB), :])
                        total[c] = term if total[c] is None else total[c] + term
                zz = (tile % 2) * (SUB // NCORE) + row // NCORE
                for c in range(3):
                    part[block, row % NCORE, zz, tile // 2, c] = total[c]
                part[block, row % NCORE, zz, tile // 2, 3] = clear
            return tuple(shadow)

        one = jnp.ones((SUB, LANES), jnp.float32)
        lax.fori_loop(0, tiles_a, second, (one,) * layers)
        core_copy(block).start()
        if block:
            join_cores(block - 1)
    join_cores(blocks - 1)

    for block in range(blocks):
        join_pair(block)

    for block in range(blocks):
        for i in range(1, half):
            q = (pair + i) % half
            pltpu.make_async_copy(z_in.at[block, q], z_in.at[block, q], z_recv.at[block, q]).wait()

        @pl.loop(0, ny)
        def _(yy):
            total = [z_in[block, 0, yy, k] for k in range(4)]
            for i in range(1, half):
                total = over(total, [z_in[block, i, yy, k] for k in range(4)])
            for k in range(4):
                y_part[block, yy, k] = total[k]

        for d in range(1, ny):
            y_copy(block, d).start()
        for k in range(4):
            y_in[block, y, k] = y_part[block, y, k]

    for block in range(blocks):
        for i in range(1, ny):
            yy = (y + i) % ny
            pltpu.make_async_copy(y_in.at[block, yy], y_in.at[block, yy], y_recv.at[block, yy]).wait()
        total = [y_in[block, 0, k] for k in range(4)]
        for i in range(1, ny):
            total = over(total, [y_in[block, i, k] for k in range(4)])
        for k in range(4):
            out_ref[k, pl.ds(block * SUB, SUB)] = total[k]

    for block in range(blocks):
        for d in range(1, nx):

            @pl.when(x + d < nx)
            def _(d=d, block=block):
                pltpu.make_async_copy(leave.at[block], leave.at[block], leave_send.at[d, block]).wait()

        core_copy(block).wait_send()
        for j in range(half):
            pair_copy(block, j).wait_send()
        for j in range(1, half):
            z_copy(block, j).wait_send()
        for d in range(1, ny):
            y_copy(block, d).wait_send()


def local(density, tables, table_index, light_code, light_tint):
    layers, slices, columns = density.shape
    nx, ny = lax.axis_size("light"), lax.axis_size("view") // (NZ * NCORE)
    table_count, _, knots = tables.shape
    tiles = columns // LANES
    blocks = tiles // SUB
    tiled = density.reshape(layers, slices // SUB, SUB, tiles, LANES).transpose(0, 1, 3, 2, 4)
    tiled = tiled.reshape(layers, slices // SUB, tiles * SUB, LANES)
    f32 = jnp.float32
    image = pl.pallas_call(
        functools.partial(kernel, nx, ny, layers, slices, columns, knots, table_count, light_code.shape[0]),
        out_shape=jax.ShapeDtypeStruct((4, tiles, LANES), f32),
        in_specs=[pl.BlockSpec(memory_space=pltpu.SMEM)] * 3
        + [pl.BlockSpec(memory_space=pltpu.VMEM), pl.BlockSpec(memory_space=pl.ANY)],
        out_specs=pl.BlockSpec(memory_space=pltpu.VMEM),
        scratch_shapes=[
            pltpu.VMEM((blocks, layers, slices // SUB, SUB * SUB, LANES), f32),
            pltpu.VMEM((blocks, slices, layers, SUB, LANES), f32),
            pltpu.VMEM((blocks, slices, layers, SUB, LANES), jnp.int32),
            pltpu.VMEM((blocks, slices, layers, SUB, LANES), f32),
            pltpu.VMEM((SUB, LANES), f32),
            pltpu.VMEM((blocks, layers * SUB, LANES), f32),
            pltpu.VMEM((nx, blocks, layers * SUB, LANES), f32),
            pltpu.VMEM((3, layers, columns), f32),
            pltpu.VMEM((3, blocks, layers * SUB, LANES), f32),
            pltpu.VMEM((blocks, NCORE, NZ, ny, 4, SUB, LANES), f32),
            pltpu.VMEM((blocks, NZ, ny, 4, SUB, LANES), f32),
            pltpu.VMEM((blocks, NZ // 2, ny, 4, SUB, LANES), f32),
            pltpu.VMEM((blocks, NZ // 2, ny, 4, SUB, LANES), f32),
            pltpu.VMEM((blocks, ny, 4, SUB, LANES), f32),
            pltpu.VMEM((blocks, ny, 4, SUB, LANES), f32),
            pltpu.SemaphoreType.DMA((blocks,)),
            pltpu.SemaphoreType.DMA((nx, blocks)),
            pltpu.SemaphoreType.DMA((nx, blocks)),
            pltpu.SemaphoreType.DMA((blocks,)),
            pltpu.SemaphoreType.DMA((blocks,)),
            pltpu.SemaphoreType.DMA((blocks, NZ // 2)),
            pltpu.SemaphoreType.DMA((blocks, NZ // 2)),
            pltpu.SemaphoreType.DMA((blocks, NZ // 2)),
            pltpu.SemaphoreType.DMA((blocks, NZ // 2)),
            pltpu.SemaphoreType.DMA((blocks, ny)),
            pltpu.SemaphoreType.DMA((blocks, ny)),
        ],
        compiler_params=pltpu.CompilerParams(
            collective_id=0, has_side_effects=True, vmem_limit_bytes=60 * 1024 * 1024
        ),
    )(table_index, light_code, light_tint, tables, tiled)
    return image.reshape(4, 1, columns)


def solution(mesh):
    return jax.shard_map(
        local,
        mesh=mesh,
        in_specs=(P("view", "light", None), P(), P("light", "view"), P(), P()),
        out_specs=P(None, ("light", "view"), None),
        check_vma=False,
    )
```

```python
import functools
import math

import jax
import jax.numpy as jnp
from jax import lax
from jax.experimental import pallas as pl
from jax.experimental.pallas import tpu as pltpu
from jax.sharding import PartitionSpec as P

MESH = pl.DeviceIdType.MESH
LANES = 128
SUB = 8
NZ, NCORE = 8, 2


def take(table, index, axis):
    numbers = lax.GatherDimensionNumbers(
        offset_dims=(), collapsed_slice_dims=(axis,), start_index_map=(axis,),
        operand_batching_dims=(1 - axis,), start_indices_batching_dims=(1 - axis,),
    )
    return lax.gather(
        table, index[:, :, None], numbers, (1, 1), mode=lax.GatherScatterMode.PROMISE_IN_BOUNDS
    )


def over(front, back):
    out = [front[k] + front[3] * back[k] for k in range(3)]
    return out + [front[3] * back[3]]


def kernel(
    nx, ny, layers, slices, columns, knots, table_count, lights,
    index_ref, code_ref, tint_ref, tables_ref, density_ref, out_ref,
    dens, cells, knot, keep, tab, leave, leave_in, fronts, light, shades,
    part, core_in, up_in, down_in, cross_in, y_part, y_in, rest, rest_in,
    dens_sem, leave_send, leave_recv, core_send, core_recv, up_send, up_recv, down_send, down_recv,
    cross_send, cross_recv, y_send, y_recv, rest_send, rest_recv,
):
    x = lax.axis_index("light")
    v = lax.axis_index("view")
    core = v % NCORE
    z = (v // NCORE) % NZ
    y = v // (NCORE * NZ)
    blocks = columns // (SUB * LANES)
    tiles_a = slices // SUB
    tiles = columns // LANES

    def at_view(yy, zz, cc):
        return {"view": (yy * NZ + zz) * NCORE + cc}

    for block in range(blocks):
        pltpu.make_async_copy(
            density_ref.at[:, :, pl.ds(block * SUB * SUB, SUB * SUB)], dens.at[block], dens_sem.at[block]
        ).start()

    barrier = pltpu.get_barrier_semaphore()
    peers = [at_view(y, z, 1 - core)]
    peers += [at_view(y, (z + d) % NZ, core) for d in (1, NZ - 1)]
    peers += [at_view((y + d) % ny, z, core) for d in range(1, ny)]
    peers += [{"light": (x + d) % nx} for d in range(1, nx)]
    for peer in peers:
        pl.semaphore_signal(barrier, inc=1, device_id=peer, device_id_type=MESH)

    chosen = tables_ref[index_ref[0, 0]]
    tab[...] = jnp.zeros_like(tab)
    tab[0:4, 0:knots] = chosen
    knot_values = tab[...]
    lane = lax.broadcasted_iota(jnp.int32, (SUB, LANES), 1)
    rise = jnp.where(lane < knots - 1, pltpu.roll(knot_values, LANES - 1, 1) - knot_values, 0.0)
    base = knot_values - rise * lane.astype(jnp.float32)
    depth_scale = -math.log2(math.e) * math.exp2(-9)

    def along_lanes(table, q):
        return jnp.broadcast_to(table[q : q + 1], (SUB, LANES))

    def along_sublanes(table, q):
        sublane = lax.broadcasted_iota(jnp.int32, (SUB, LANES), 0)
        halves = []
        for first_knot in (0, SUB):
            picked = jnp.where(lane == sublane + first_knot, along_lanes(table, q), 0.0)
            halves.append(jnp.broadcast_to(jnp.sum(picked, axis=1, keepdims=True), (SUB, LANES)))
        return halves

    split = [(along_sublanes(base * s, q), along_sublanes(rise * s, q)) for q, s in ((0, depth_scale), (1, 1.0), (2, 1.0))]
    whole = along_lanes(base, 3), along_lanes(rise, 3)

    def level(q, scaled, k):
        if q == 3:
            return take(whole[0], k, 1) + take(whole[1], k, 1) * scaled
        low = k & (SUB - 1)
        parts = [jnp.where(scaled >= float(SUB), take(t[1], low, 0), take(t[0], low, 0)) for t in split[q]]
        return parts[0] + parts[1] * scaled

    for block in range(blocks):
        pltpu.make_async_copy(dens.at[block], dens.at[block], dens_sem.at[block]).wait()

        def first(tile, sums, block=block):
            sums = list(sums)
            for row in range(SUB):
                for b in range(layers):
                    scaled = dens[block, b, tile, pl.ds(row, SUB, stride=SUB), :] * float(knots - 1)
                    k = scaled.astype(jnp.int32)
                    depth = level(0, scaled, k)
                    keep[block, tile * SUB + row, b] = jnp.exp2(depth)
                    cells[block, tile * SUB + row, b] = scaled
                    knot[block, tile * SUB + row, b] = k
                    sums[b] = sums[b] + depth
            return tuple(sums)

        zero = jnp.zeros((SUB, LANES), jnp.float32)
        sums = lax.fori_loop(0, tiles_a, first, (zero,) * layers)
        for b in range(layers):
            leave[block, pl.ds(b * SUB, SUB)] = jnp.exp2(sums[b] * 2.0)
        if block == 0:
            pl.semaphore_wait(barrier, len(peers))
        for d in range(1, nx):

            @pl.when(x + d < nx)
            def _(d=d, block=block):
                pltpu.make_async_remote_copy(
                    src_ref=leave.at[block], dst_ref=leave_in.at[x, block],
                    send_sem=leave_send.at[d, block], recv_sem=leave_recv.at[x, block],
                    device_id={"light": (x + d) % nx}, device_id_type=MESH,
                ).start()

    column = lax.broadcasted_iota(jnp.int32, (layers, columns), 1)
    fronts[...] = jnp.ones_like(fronts)

    def moved(values, by):
        rolled = pltpu.roll(values, by % columns, 1)
        inside = column >= by if by > 0 else column < columns + by
        return jnp.where(inside, rolled, 0.0)

    for stage in range(nx - 1):

        @pl.when(x > stage)
        def _(stage=stage):
            for block in range(blocks):
                pltpu.make_async_copy(
                    leave_in.at[stage, block], leave_in.at[stage, block], leave_recv.at[stage, block]
                ).wait()
            gone = jnp.concatenate(
                [leave_in[stage, t // SUB, pl.ds(t % SUB, layers, stride=SUB), :] for t in range(tiles)], axis=1
            )
            for drift in (-1, 0, 1):
                value = fronts[drift + 1] * gone
                total = 0.0
                for offset, share in ((drift - 1, 0.25), (drift, 0.5), (drift + 1, 0.25)):
                    total = total + share * (moved(value, offset) if offset else value)
                fronts[drift + 1] = total

    for k in range(3):
        tint = [0.0, 0.0, 0.0]
        for l in range(lights):
            for drift in (-1, 0, 1):
                tint[drift + 1] = tint[drift + 1] + jnp.where(code_ref[l] == drift, tint_ref[l, k], 0.0)
        for t in range(tiles):
            cols = pl.ds(t * LANES, LANES)
            light[k, t // SUB, pl.ds(t % SUB, layers, stride=SUB), :] = (
                fronts[0, :, cols] * tint[0] + fronts[1, :, cols] * tint[1] + fronts[2, :, cols] * tint[2]
            )

    pieces = blocks * ny
    quad = NZ // 2
    half = z // quad
    q = z % quad
    last = quad - 1
    up_base = half * quad
    down_base = quad - up_base
    own_base = (z + NZ - 2 - q // last) % NZ
    toward = 2 * (q // last) - 1
    own = q // last

    def core_copy(n):
        return pltpu.make_async_remote_copy(
            src_ref=part.at[n, 1 - core], dst_ref=core_in.at[n],
            send_sem=core_send.at[n], recv_sem=core_recv.at[n],
            device_id=at_view(y, z, 1 - core), device_id_type=MESH,
        )

    def up_copy(n):
        return pltpu.make_async_remote_copy(
            src_ref=part.at[n, core, pl.ds(up_base, quad)], dst_ref=up_in.at[n],
            send_sem=up_send.at[n], recv_sem=up_recv.at[n],
            device_id=at_view(y, (z + 1) % NZ, core), device_id_type=MESH,
        )

    def down_copy(n):
        return pltpu.make_async_remote_copy(
            src_ref=part.at[n, core, pl.ds(down_base, quad)], dst_ref=down_in.at[n],
            send_sem=down_send.at[n], recv_sem=down_recv.at[n],
            device_id=at_view(y, (z + NZ - 1) % NZ, core), device_id_type=MESH,
        )

    def cross_copy(n):
        return pltpu.make_async_remote_copy(
            src_ref=part.at[n, core, pl.ds((own_base + 2 * toward + NZ) % NZ, 2)], dst_ref=cross_in.at[n],
            send_sem=cross_send.at[n], recv_sem=cross_recv.at[n],
            device_id=at_view(y, (z + toward + NZ) % NZ, core), device_id_type=MESH,
        )

    def y_copy(n, to, source):
        return pltpu.make_async_remote_copy(
            src_ref=y_part.at[n], dst_ref=y_in.at[n // ny, source],
            send_sem=y_send.at[n], recv_sem=y_recv.at[n // ny, source],
            device_id=at_view(to, z, core), device_id_type=MESH,
        )

    def rest_copy(block):
        return pltpu.make_async_remote_copy(
            src_ref=rest.at[block], dst_ref=rest_in.at[block],
            send_sem=rest_send.at[block], recv_sem=rest_recv.at[block],
            device_id=at_view(y, (z - toward + NZ) % NZ, core), device_id_type=MESH,
        )

    is_end = jnp.logical_or(q == 0, q == last)

    def ordered(later, mine, other):
        front = [jnp.where(later, o, m) for m, o in zip(mine, other)]
        back = [jnp.where(later, m, o) for m, o in zip(mine, other)]
        return over(front, back)

    def second(n):
        block, yy = n // ny, n % ny

        @pl.when(yy == 0)
        def _():
            shades[...] = jnp.ones_like(shades)

        def rows(i, shadow):
            shadow = list(shadow)
            tile = yy * 2 + i
            for row in range(SUB):
                clear = None
                total = [None] * 3
                for b in range(layers):
                    scaled = cells[block, tile * SUB + row, b]
                    k = knot[block, tile * SUB + row, b]
                    stays = keep[block, tile * SUB + row, b]
                    if clear is None:
                        weight = (1.0 - stays) * shadow[b]
                        clear = stays
                    else:
                        after = clear * stays
                        weight = (clear - after) * shadow[b]
                        clear = after
                    shadow[b] = shadow[b] * (stays * stays)
                    for c in range(3):
                        color = level(c + 1, scaled, k)
                        term = color * (weight * light[c, block, pl.ds(b * SUB, SUB), :])
                        total[c] = term if total[c] is None else total[c] + term
                slot = (i * (SUB // NCORE) + row // NCORE + NZ - 2) % NZ
                for c in range(3):
                    part[n, row % NCORE, slot, c] = total[c]
                part[n, row % NCORE, slot, 3] = clear
            return tuple(shadow)

        shadow = lax.fori_loop(0, 2, rows, tuple(shades[b] for b in range(layers)))
        for b in range(layers):
            shades[b] = shadow[b]

    def join(n, first, count, incoming, later):
        for i in range(count):
            mine = [part[n, core, first + i, k] for k in range(4)]
            joined = ordered(later, mine, [incoming[n, i, k] for k in range(4)])
            for k in range(4):
                part[n, core, first + i, k] = joined[k]

    def due(n):
        return jnp.logical_and(n >= 0, n < pieces)

    core_lag, hop_lag, y_lag = 2, 3, 2
    steps = pieces + core_lag + last * hop_lag + hop_lag + y_lag

    @pl.loop(0, steps)
    def _(step):
        @pl.when(step < pieces)
        def _():
            second(step)
            core_copy(step).start()

        at = step - core_lag

        @pl.when(due(at))
        def _():
            core_copy(at).wait_recv()
            join(at, 0, NZ, core_in, core == 1)

            @pl.when(q == 0)
            def _():
                up_copy(at).start()

            @pl.when(q == last)
            def _():
                down_copy(at).start()

        up_at = at - hop_lag * q

        @pl.when(jnp.logical_and(due(up_at), q > 0))
        def _():
            up_copy(up_at).wait_recv()
            join(up_at, up_base, quad, up_in, q > 0)

            @pl.when(q < last)
            def _():
                up_copy(up_at).start()

            @pl.when(q == last)
            def _():
                cross_copy(up_at).start()

        down_at = at - hop_lag * (last - q)

        @pl.when(jnp.logical_and(due(down_at), q < last))
        def _():
            down_copy(down_at).wait_recv()
            join(down_at, down_base, quad, down_in, q < 0)

            @pl.when(q > 0)
            def _():
                down_copy(down_at).start()

            @pl.when(q == 0)
            def _():
                cross_copy(down_at).start()

        cross_at = at - hop_lag * last - hop_lag

        @pl.when(jnp.logical_and(due(cross_at), is_end))
        def _():
            cross_copy(cross_at).wait_recv()
            to = cross_at % ny
            for i in range(2):
                mine = [part[cross_at, core, own_base + i, k] for k in range(4)]
                joined = ordered(half == 1, mine, [cross_in[cross_at, i, k] for k in range(4)])
                for k in range(4):
                    y_part[cross_at, i, k] = joined[k]

            @pl.when(to != y)
            def _():
                y_copy(cross_at, to, y).start()

        y_at = cross_at - y_lag

        @pl.when(jnp.logical_and(jnp.logical_and(due(y_at), is_end), y_at % ny == y))
        def _():
            block = y_at // ny
            for i in range(1, ny):
                source = (y + i) % ny
                y_copy(y_at, source, source).wait_recv()
            for i in range(2):
                for k in range(4):
                    y_in[block, y, i, k] = y_part[y_at, i, k]
            for i in range(2):
                total = [y_in[block, 0, i, k] for k in range(4)]
                for j in range(1, ny):
                    total = over(total, [y_in[block, j, i, k] for k in range(4)])

                @pl.when(own == i)
                def _():
                    for k in range(4):
                        out_ref[k, pl.ds(block * SUB, SUB)] = total[k]

                @pl.when(own != i)
                def _():
                    for k in range(4):
                        rest[block, k] = total[k]

            rest_copy(block).start()

    @pl.when(jnp.logical_not(is_end))
    def _():
        for block in range(blocks):
            rest_copy(block).wait_recv()
            for k in range(4):
                out_ref[k, pl.ds(block * SUB, SUB)] = rest_in[block, k]

    for block in range(blocks):
        for d in range(1, nx):

            @pl.when(x + d < nx)
            def _(d=d, block=block):
                pltpu.make_async_copy(leave.at[block], leave.at[block], leave_send.at[d, block]).wait()

    @pl.loop(0, pieces)
    def _(n):
        core_copy(n).wait_send()

        @pl.when(q < last)
        def _():
            up_copy(n).wait_send()

        @pl.when(q > 0)
        def _():
            down_copy(n).wait_send()

        @pl.when(is_end)
        def _():
            cross_copy(n).wait_send()

            @pl.when(n % ny != y)
            def _():
                y_copy(n, n % ny, y).wait_send()

    @pl.when(is_end)
    def _():
        for block in range(blocks):
            rest_copy(block).wait_send()


def local(density, tables, table_index, light_code, light_tint):
    layers, slices, columns = density.shape
    nx, ny = lax.axis_size("light"), lax.axis_size("view") // (NZ * NCORE)
    table_count, _, knots = tables.shape
    tiles = columns // LANES
    blocks = tiles // SUB
    tiled = density.reshape(layers, slices // SUB, SUB, tiles, LANES).transpose(0, 1, 3, 2, 4)
    tiled = tiled.reshape(layers, slices // SUB, tiles * SUB, LANES)
    pieces = blocks * ny
    f32 = jnp.float32
    image = pl.pallas_call(
        functools.partial(kernel, nx, ny, layers, slices, columns, knots, table_count, light_code.shape[0]),
        out_shape=jax.ShapeDtypeStruct((4, tiles, LANES), f32),
        in_specs=[pl.BlockSpec(memory_space=pltpu.SMEM)] * 3
        + [pl.BlockSpec(memory_space=pltpu.VMEM), pl.BlockSpec(memory_space=pl.ANY)],
        out_specs=pl.BlockSpec(memory_space=pltpu.VMEM),
        scratch_shapes=[
            pltpu.VMEM((blocks, layers, slices // SUB, SUB * SUB, LANES), f32),
            pltpu.VMEM((blocks, slices, layers, SUB, LANES), f32),
            pltpu.VMEM((blocks, slices, layers, SUB, LANES), jnp.int32),
            pltpu.VMEM((blocks, slices, layers, SUB, LANES), f32),
            pltpu.VMEM((SUB, LANES), f32),
            pltpu.VMEM((blocks, layers * SUB, LANES), f32),
            pltpu.VMEM((nx, blocks, layers * SUB, LANES), f32),
            pltpu.VMEM((3, layers, columns), f32),
            pltpu.VMEM((3, blocks, layers * SUB, LANES), f32),
            pltpu.VMEM((layers, SUB, LANES), f32),
            pltpu.VMEM((pieces, NCORE, NZ, 4, SUB, LANES), f32),
            pltpu.VMEM((pieces, NZ, 4, SUB, LANES), f32),
            pltpu.VMEM((pieces, NZ // 2, 4, SUB, LANES), f32),
            pltpu.VMEM((pieces, NZ // 2, 4, SUB, LANES), f32),
            pltpu.VMEM((pieces, 2, 4, SUB, LANES), f32),
            pltpu.VMEM((pieces, 2, 4, SUB, LANES), f32),
            pltpu.VMEM((blocks, ny, 2, 4, SUB, LANES), f32),
            pltpu.VMEM((blocks, 4, SUB, LANES), f32),
            pltpu.VMEM((blocks, 4, SUB, LANES), f32),
            pltpu.SemaphoreType.DMA((blocks,)),
            pltpu.SemaphoreType.DMA((nx, blocks)),
            pltpu.SemaphoreType.DMA((nx, blocks)),
        ]
        + [pltpu.SemaphoreType.DMA((pieces,))] * 9
        + [
            pltpu.SemaphoreType.DMA((blocks, ny)),
            pltpu.SemaphoreType.DMA((blocks,)),
            pltpu.SemaphoreType.DMA((blocks,)),
        ],
        compiler_params=pltpu.CompilerParams(
            collective_id=0, has_side_effects=True, vmem_limit_bytes=60 * 1024 * 1024
        ),
    )(table_index, light_code, light_tint, tables, tiled)
    return image.reshape(4, 1, columns)


def solution(mesh):
    return jax.shard_map(
        local,
        mesh=mesh,
        in_specs=(P("view", "light", None), P(), P("light", "view"), P(), P()),
        out_specs=P(None, ("light", "view"), None),
        check_vma=False,
    )
```

```python
import functools
import math

import jax
import jax.numpy as jnp
from jax import lax
from jax.experimental import pallas as pl
from jax.experimental.pallas import tpu as pltpu
from jax.sharding import PartitionSpec as P

MESH = pl.DeviceIdType.MESH
LANES = 128
SUB = 8
NZ, NCORE = 8, 2


def take(table, index, axis):
    numbers = lax.GatherDimensionNumbers(
        offset_dims=(), collapsed_slice_dims=(axis,), start_index_map=(axis,),
        operand_batching_dims=(1 - axis,), start_indices_batching_dims=(1 - axis,),
    )
    return lax.gather(
        table, index[:, :, None], numbers, (1, 1), mode=lax.GatherScatterMode.PROMISE_IN_BOUNDS
    )


def over(front, back):
    out = [front[k] + front[3] * back[k] for k in range(3)]
    return out + [front[3] * back[3]]


def kernel(
    nx, ny, layers, slices, columns, knots, table_count, lights,
    index_ref, code_ref, tint_ref, tables_ref, density_ref, out_ref,
    dens, cells, knot, keep, tab, leave, leave_in, fronts, light, shades,
    part, core_in, up_in, down_in, cross_in, y_part, y_in, rest, rest_in,
    dens_sem, leave_send, leave_recv, core_send, core_recv, up_send, up_recv, down_send, down_recv,
    cross_send, cross_recv, y_send, y_recv, rest_send, rest_recv,
):
    x = lax.axis_index("light")
    v = lax.axis_index("view")
    core = v % NCORE
    z = (v // NCORE) % NZ
    y = v // (NCORE * NZ)
    blocks = columns // (SUB * LANES)
    tiles_a = slices // SUB
    tiles = columns // LANES

    def at_view(yy, zz, cc):
        return {"view": (yy * NZ + zz) * NCORE + cc}

    for block in range(blocks):
        pltpu.make_async_copy(
            density_ref.at[:, :, pl.ds(block * SUB * SUB, SUB * SUB)], dens.at[block], dens_sem.at[block]
        ).start()

    barrier = pltpu.get_barrier_semaphore()
    peers = [at_view(y, z, 1 - core)]
    peers += [at_view(y, (z + d) % NZ, core) for d in (1, NZ - 1)]
    peers += [at_view((y + d) % ny, z, core) for d in range(1, ny)]
    peers += [{"light": (x + d) % nx} for d in range(1, nx)]
    for peer in peers:
        pl.semaphore_signal(barrier, inc=1, device_id=peer, device_id_type=MESH)

    chosen = tables_ref[index_ref[0, 0]]
    tab[...] = jnp.zeros_like(tab)
    tab[0:4, 0:knots] = chosen
    knot_values = tab[...]
    lane = lax.broadcasted_iota(jnp.int32, (SUB, LANES), 1)
    rise = jnp.where(lane < knots - 1, pltpu.roll(knot_values, LANES - 1, 1) - knot_values, 0.0)
    base = knot_values - rise * lane.astype(jnp.float32)
    depth_scale = -math.log2(math.e) * math.exp2(-9)

    def along_lanes(table, q):
        return jnp.broadcast_to(table[q : q + 1], (SUB, LANES))

    def along_sublanes(table, q):
        sublane = lax.broadcasted_iota(jnp.int32, (SUB, LANES), 0)
        halves = []
        for first_knot in (0, SUB):
            picked = jnp.where(lane == sublane + first_knot, along_lanes(table, q), 0.0)
            halves.append(jnp.broadcast_to(jnp.sum(picked, axis=1, keepdims=True), (SUB, LANES)))
        return halves

    split = [(along_sublanes(base * s, q), along_sublanes(rise * s, q)) for q, s in ((0, depth_scale), (1, 1.0), (2, 1.0))]
    whole = along_lanes(base, 3), along_lanes(rise, 3)

    def level(q, scaled, k):
        if q == 3:
            return take(whole[0], k, 1) + take(whole[1], k, 1) * scaled
        low = k & (SUB - 1)
        parts = [jnp.where(scaled >= float(SUB), take(t[1], low, 0), take(t[0], low, 0)) for t in split[q]]
        return parts[0] + parts[1] * scaled

    def leave_copy(block, d):
        return pltpu.make_async_remote_copy(
            src_ref=leave.at[block], dst_ref=leave_in.at[x, block],
            send_sem=leave_send.at[d, block], recv_sem=leave_recv.at[x, block],
            device_id={"light": (x + d) % nx}, device_id_type=MESH,
        )

    def first(block):
        pltpu.make_async_copy(dens.at[block], dens.at[block], dens_sem.at[block]).wait()

        def rows(tile, sums):
            sums = list(sums)
            for row in range(SUB):
                for b in range(layers):
                    scaled = dens[block, b, tile, pl.ds(row, SUB, stride=SUB), :] * float(knots - 1)
                    k = scaled.astype(jnp.int32)
                    depth = level(0, scaled, k)
                    keep[block, tile * SUB + row, b] = jnp.exp2(depth)
                    cells[block, tile * SUB + row, b] = scaled
                    knot[block, tile * SUB + row, b] = k
                    sums[b] = sums[b] + depth
            return tuple(sums)

        zero = jnp.zeros((SUB, LANES), jnp.float32)
        sums = lax.fori_loop(0, tiles_a, rows, (zero,) * layers)
        for b in range(layers):
            leave[block, pl.ds(b * SUB, SUB)] = jnp.exp2(sums[b] * 2.0)
        if block == 0:
            pl.semaphore_wait(barrier, len(peers))
        for d in range(1, nx):

            @pl.when(x + d < nx)
            def _(d=d):
                leave_copy(block, d).start()

    wide = (SUB + 2) * LANES

    def light_up(block):
        fronts[...] = jnp.ones_like(fronts)
        before = jnp.maximum(block - 1, 0)
        behind = jnp.minimum(block + 1, blocks - 1)
        for stage in range(nx - 1):

            @pl.when(x > stage)
            def _(stage=stage):
                def gone_of(at, t):
                    return leave_in[stage, at, pl.ds(t, layers, stride=SUB), :]

                gone = [jnp.where(block > 0, gone_of(before, SUB - 1), 0.0)]
                gone += [gone_of(block, t) for t in range(SUB)]
                gone += [jnp.where(block < blocks - 1, gone_of(behind, 0), 0.0)]
                gone = jnp.concatenate(gone, axis=1)
                for drift in (-1, 0, 1):
                    value = fronts[drift + 1] * gone
                    sides = pltpu.roll(value, (drift - 1) % wide, 1) if drift != 1 else value
                    sides = sides + (pltpu.roll(value, (drift + 1) % wide, 1) if drift != -1 else value)
                    center = pltpu.roll(value, drift % wide, 1) if drift else value
                    fronts[drift + 1] = 0.25 * sides + 0.5 * center

        for k in range(3):
            tint = [0.0, 0.0, 0.0]
            for l in range(lights):
                for drift in (-1, 0, 1):
                    tint[drift + 1] = tint[drift + 1] + jnp.where(code_ref[l] == drift, tint_ref[l, k], 0.0)
            for t in range(SUB):
                cols = pl.ds((t + 1) * LANES, LANES)
                light[k, block, pl.ds(t, layers, stride=SUB), :] = (
                    fronts[0, :, cols] * tint[0] + fronts[1, :, cols] * tint[1] + fronts[2, :, cols] * tint[2]
                )

    def leaves_arrive(block):
        for stage in range(nx - 1):

            @pl.when(x > stage)
            def _(stage=stage):
                pltpu.make_async_copy(
                    leave_in.at[stage, block], leave_in.at[stage, block], leave_recv.at[stage, block]
                ).wait()

    pieces = blocks * ny
    quad = NZ // 2
    half = z // quad
    q = z % quad
    last = quad - 1
    up_base = half * quad
    down_base = quad - up_base
    own_base = (z + NZ - 2 - q // last) % NZ
    toward = 2 * (q // last) - 1
    own = q // last

    def core_copy(n):
        return pltpu.make_async_remote_copy(
            src_ref=part.at[n, 1 - core], dst_ref=core_in.at[n],
            send_sem=core_send.at[n], recv_sem=core_recv.at[n],
            device_id=at_view(y, z, 1 - core), device_id_type=MESH,
        )

    def up_copy(n):
        return pltpu.make_async_remote_copy(
            src_ref=part.at[n, core, pl.ds(up_base, quad)], dst_ref=up_in.at[n],
            send_sem=up_send.at[n], recv_sem=up_recv.at[n],
            device_id=at_view(y, (z + 1) % NZ, core), device_id_type=MESH,
        )

    def down_copy(n):
        return pltpu.make_async_remote_copy(
            src_ref=part.at[n, core, pl.ds(down_base, quad)], dst_ref=down_in.at[n],
            send_sem=down_send.at[n], recv_sem=down_recv.at[n],
            device_id=at_view(y, (z + NZ - 1) % NZ, core), device_id_type=MESH,
        )

    def cross_copy(n):
        return pltpu.make_async_remote_copy(
            src_ref=part.at[n, core, pl.ds((own_base + 2 * toward + NZ) % NZ, 2)], dst_ref=cross_in.at[n],
            send_sem=cross_send.at[n], recv_sem=cross_recv.at[n],
            device_id=at_view(y, (z + toward + NZ) % NZ, core), device_id_type=MESH,
        )

    def y_copy(n, to, source):
        return pltpu.make_async_remote_copy(
            src_ref=y_part.at[n], dst_ref=y_in.at[n // ny, source],
            send_sem=y_send.at[n], recv_sem=y_recv.at[n // ny, source],
            device_id=at_view(to, z, core), device_id_type=MESH,
        )

    def rest_copy(block):
        return pltpu.make_async_remote_copy(
            src_ref=rest.at[block], dst_ref=rest_in.at[block],
            send_sem=rest_send.at[block], recv_sem=rest_recv.at[block],
            device_id=at_view(y, (z - toward + NZ) % NZ, core), device_id_type=MESH,
        )

    is_end = jnp.logical_or(q == 0, q == last)

    def ordered(later, mine, other):
        front = [jnp.where(later, o, m) for m, o in zip(mine, other)]
        back = [jnp.where(later, m, o) for m, o in zip(mine, other)]
        return over(front, back)

    def second(n):
        block, yy = n // ny, n % ny

        @pl.when(yy == 0)
        def _():
            shades[...] = jnp.ones_like(shades)

        def rows(i, shadow):
            shadow = list(shadow)
            tile = yy * 2 + i
            for row in range(SUB):
                clear = None
                total = [None] * 3
                for b in range(layers):
                    scaled = cells[block, tile * SUB + row, b]
                    k = knot[block, tile * SUB + row, b]
                    stays = keep[block, tile * SUB + row, b]
                    if clear is None:
                        weight = (1.0 - stays) * shadow[b]
                        clear = stays
                    else:
                        after = clear * stays
                        weight = (clear - after) * shadow[b]
                        clear = after
                    shadow[b] = shadow[b] * (stays * stays)
                    for c in range(3):
                        color = level(c + 1, scaled, k)
                        term = color * (weight * light[c, block, pl.ds(b * SUB, SUB), :])
                        total[c] = term if total[c] is None else total[c] + term
                slot = (i * (SUB // NCORE) + row // NCORE + NZ - 2) % NZ
                for c in range(3):
                    part[n, row % NCORE, slot, c] = total[c]
                part[n, row % NCORE, slot, 3] = clear
            return tuple(shadow)

        shadow = lax.fori_loop(0, 2, rows, tuple(shades[b] for b in range(layers)))
        for b in range(layers):
            shades[b] = shadow[b]

    def join(n, first, count, incoming, later):
        for i in range(count):
            mine = [part[n, core, first + i, k] for k in range(4)]
            joined = ordered(later, mine, [incoming[n, i, k] for k in range(4)])
            for k in range(4):
                part[n, core, first + i, k] = joined[k]

    def due(n):
        return jnp.logical_and(n >= 0, n < pieces)

    core_lag, hop_lag, cross_lag, y_lag = 1, 3, 6, 6
    steps = pieces + core_lag + last * hop_lag + cross_lag + y_lag

    ahead = blocks - 1
    for block in range(ahead):
        first(block)

    @pl.loop(0, steps)
    def _(step):
        @pl.when(step == 1)
        def _():
            for block in range(ahead, blocks):
                first(block)

        @pl.when(jnp.logical_and(step % ny == 0, step < pieces))
        def _():
            block = step // ny

            @pl.when(block == 0)
            def _():
                leaves_arrive(0)

            @pl.when(block < blocks - 1)
            def _():
                leaves_arrive(block + 1)

            light_up(block)

        @pl.when(step < pieces)
        def _():
            second(step)
            core_copy(step).start()

        at = step - core_lag

        @pl.when(due(at))
        def _():
            core_copy(at).wait_recv()
            join(at, 0, NZ, core_in, core == 1)

            @pl.when(q == 0)
            def _():
                up_copy(at).start()

            @pl.when(q == last)
            def _():
                down_copy(at).start()

        up_at = at - hop_lag * q

        @pl.when(jnp.logical_and(due(up_at), q > 0))
        def _():
            up_copy(up_at).wait_recv()
            join(up_at, up_base, quad, up_in, q > 0)

            @pl.when(q < last)
            def _():
                up_copy(up_at).start()

            @pl.when(q == last)
            def _():
                cross_copy(up_at).start()

        down_at = at - hop_lag * (last - q)

        @pl.when(jnp.logical_and(due(down_at), q < last))
        def _():
            down_copy(down_at).wait_recv()
            join(down_at, down_base, quad, down_in, q < 0)

            @pl.when(q > 0)
            def _():
                down_copy(down_at).start()

            @pl.when(q == 0)
            def _():
                cross_copy(down_at).start()

        cross_at = at - hop_lag * last - cross_lag

        @pl.when(jnp.logical_and(due(cross_at), is_end))
        def _():
            cross_copy(cross_at).wait_recv()
            to = cross_at % ny
            for i in range(2):
                mine = [part[cross_at, core, own_base + i, k] for k in range(4)]
                joined = ordered(half == 1, mine, [cross_in[cross_at, i, k] for k in range(4)])
                for k in range(4):
                    y_part[cross_at, i, k] = joined[k]

            @pl.when(to != y)
            def _():
                y_copy(cross_at, to, y).start()

        y_at = cross_at - y_lag

        @pl.when(jnp.logical_and(jnp.logical_and(due(y_at), is_end), y_at % ny == y))
        def _():
            block = y_at // ny
            for i in range(1, ny):
                source = (y + i) % ny
                y_copy(y_at, source, source).wait_recv()
            for i in range(2):
                for k in range(4):
                    y_in[block, y, i, k] = y_part[y_at, i, k]
            for i in range(2):
                total = [y_in[block, 0, i, k] for k in range(4)]
                for j in range(1, ny):
                    total = over(total, [y_in[block, j, i, k] for k in range(4)])

                @pl.when(own == i)
                def _():
                    for k in range(4):
                        out_ref[k, pl.ds(block * SUB, SUB)] = total[k]

                @pl.when(own != i)
                def _():
                    for k in range(4):
                        rest[block, k] = total[k]

            rest_copy(block).start()

    @pl.when(jnp.logical_not(is_end))
    def _():
        for block in range(blocks):
            rest_copy(block).wait_recv()
            for k in range(4):
                out_ref[k, pl.ds(block * SUB, SUB)] = rest_in[block, k]

    for block in range(blocks):
        for d in range(1, nx):

            @pl.when(x + d < nx)
            def _(d=d, block=block):
                leave_copy(block, d).wait_send()

    @pl.loop(0, pieces)
    def _(n):
        core_copy(n).wait_send()

        @pl.when(q < last)
        def _():
            up_copy(n).wait_send()

        @pl.when(q > 0)
        def _():
            down_copy(n).wait_send()

        @pl.when(is_end)
        def _():
            cross_copy(n).wait_send()

            @pl.when(n % ny != y)
            def _():
                y_copy(n, n % ny, y).wait_send()

    @pl.when(is_end)
    def _():
        for block in range(blocks):
            rest_copy(block).wait_send()


def local(density, tables, table_index, light_code, light_tint):
    layers, slices, columns = density.shape
    nx, ny = lax.axis_size("light"), lax.axis_size("view") // (NZ * NCORE)
    table_count, _, knots = tables.shape
    tiles = columns // LANES
    blocks = tiles // SUB
    tiled = density.reshape(layers, slices // SUB, SUB, tiles, LANES).transpose(0, 1, 3, 2, 4)
    tiled = tiled.reshape(layers, slices // SUB, tiles * SUB, LANES)
    pieces = blocks * ny
    f32 = jnp.float32
    image = pl.pallas_call(
        functools.partial(kernel, nx, ny, layers, slices, columns, knots, table_count, light_code.shape[0]),
        out_shape=jax.ShapeDtypeStruct((4, tiles, LANES), f32),
        in_specs=[pl.BlockSpec(memory_space=pltpu.SMEM)] * 3
        + [pl.BlockSpec(memory_space=pltpu.VMEM), pl.BlockSpec(memory_space=pl.ANY)],
        out_specs=pl.BlockSpec(memory_space=pltpu.VMEM),
        scratch_shapes=[
            pltpu.VMEM((blocks, layers, slices // SUB, SUB * SUB, LANES), f32),
            pltpu.VMEM((blocks, slices, layers, SUB, LANES), f32),
            pltpu.VMEM((blocks, slices, layers, SUB, LANES), jnp.int32),
            pltpu.VMEM((blocks, slices, layers, SUB, LANES), f32),
            pltpu.VMEM((SUB, LANES), f32),
            pltpu.VMEM((blocks, layers * SUB, LANES), f32),
            pltpu.VMEM((nx, blocks, layers * SUB, LANES), f32),
            pltpu.VMEM((3, layers, (SUB + 2) * LANES), f32),
            pltpu.VMEM((3, blocks, layers * SUB, LANES), f32),
            pltpu.VMEM((layers, SUB, LANES), f32),
            pltpu.VMEM((pieces, NCORE, NZ, 4, SUB, LANES), f32),
            pltpu.VMEM((pieces, NZ, 4, SUB, LANES), f32),
            pltpu.VMEM((pieces, NZ // 2, 4, SUB, LANES), f32),
            pltpu.VMEM((pieces, NZ // 2, 4, SUB, LANES), f32),
            pltpu.VMEM((pieces, 2, 4, SUB, LANES), f32),
            pltpu.VMEM((pieces, 2, 4, SUB, LANES), f32),
            pltpu.VMEM((blocks, ny, 2, 4, SUB, LANES), f32),
            pltpu.VMEM((blocks, 4, SUB, LANES), f32),
            pltpu.VMEM((blocks, 4, SUB, LANES), f32),
            pltpu.SemaphoreType.DMA((blocks,)),
            pltpu.SemaphoreType.DMA((nx, blocks)),
            pltpu.SemaphoreType.DMA((nx, blocks)),
        ]
        + [pltpu.SemaphoreType.DMA((pieces,))] * 9
        + [
            pltpu.SemaphoreType.DMA((blocks, ny)),
            pltpu.SemaphoreType.DMA((blocks,)),
            pltpu.SemaphoreType.DMA((blocks,)),
        ],
        compiler_params=pltpu.CompilerParams(
            collective_id=0, has_side_effects=True, vmem_limit_bytes=60 * 1024 * 1024
        ),
    )(table_index, light_code, light_tint, tables, tiled)
    return image.reshape(4, 1, columns)


def solution(mesh):
    return jax.shard_map(
        local,
        mesh=mesh,
        in_specs=(P("view", "light", None), P(), P("light", "view"), P(), P()),
        out_specs=P(None, ("light", "view"), None),
        check_vma=False,
    )
```

```python
import functools
import math

import jax
import jax.numpy as jnp
from jax import lax
from jax.experimental import pallas as pl
from jax.experimental.pallas import tpu as pltpu
from jax.sharding import PartitionSpec as P

MESH = pl.DeviceIdType.MESH
LANES = 128
SUB = 8
NZ, NCORE = 8, 2


def take(table, index, axis):
    numbers = lax.GatherDimensionNumbers(
        offset_dims=(), collapsed_slice_dims=(axis,), start_index_map=(axis,),
        operand_batching_dims=(1 - axis,), start_indices_batching_dims=(1 - axis,),
    )
    return lax.gather(
        table, index[:, :, None], numbers, (1, 1), mode=lax.GatherScatterMode.PROMISE_IN_BOUNDS
    )


def over(front, back):
    out = [front[k] + front[3] * back[k] for k in range(3)]
    return out + [front[3] * back[3]]


def kernel(
    nx, ny, layers, slices, columns, knots, table_count, lights,
    index_ref, code_ref, tint_ref, tables_ref, density_ref, out_ref,
    dens, cells, knot, keep, tab, leave, leave_in, fronts, light, shades,
    part, core_in, up_in, down_in, cross_in, y_part, y_in,
    dens_sem, leave_send, leave_recv, core_send, core_recv, up_send, up_recv, down_send, down_recv,
    cross_send, cross_recv, y_send, y_recv, rest_send,
):
    x = lax.axis_index("light")
    v = lax.axis_index("view")
    core = v % NCORE
    z = (v // NCORE) % NZ
    y = v // (NCORE * NZ)
    blocks = columns // (SUB * LANES)
    tiles_a = slices // SUB
    tiles = columns // LANES

    def at_view(yy, zz, cc):
        return {"view": (yy * NZ + zz) * NCORE + cc}

    for block in range(blocks):
        pltpu.make_async_copy(
            density_ref.at[:, :, pl.ds(block * SUB * SUB, SUB * SUB)], dens.at[block], dens_sem.at[block]
        ).start()

    barrier = pltpu.get_barrier_semaphore()
    peers = [at_view(y, z, 1 - core)]
    peers += [at_view(y, (z + d) % NZ, core) for d in (1, NZ - 1)]
    peers += [at_view((y + d) % ny, z, core) for d in range(1, ny)]
    peers += [at_view((y + d) % ny, z + 1 - 2 * (z % 2), core) for d in range(1, ny)]
    peers += [{"light": (x + d) % nx} for d in range(1, nx)]
    for peer in peers:
        pl.semaphore_signal(barrier, inc=1, device_id=peer, device_id_type=MESH)

    chosen = tables_ref[index_ref[0, 0]]
    tab[...] = jnp.zeros_like(tab)
    tab[0:4, 0:knots] = chosen
    knot_values = tab[...]
    lane = lax.broadcasted_iota(jnp.int32, (SUB, LANES), 1)
    rise = jnp.where(lane < knots - 1, pltpu.roll(knot_values, LANES - 1, 1) - knot_values, 0.0)
    base = knot_values - rise * lane.astype(jnp.float32)
    depth_scale = -math.log2(math.e) * math.exp2(-9)

    def along_lanes(table, q):
        return jnp.broadcast_to(table[q : q + 1], (SUB, LANES))

    def along_sublanes(table, q):
        sublane = lax.broadcasted_iota(jnp.int32, (SUB, LANES), 0)
        halves = []
        for first_knot in (0, SUB):
            picked = jnp.where(lane == sublane + first_knot, along_lanes(table, q), 0.0)
            halves.append(jnp.broadcast_to(jnp.sum(picked, axis=1, keepdims=True), (SUB, LANES)))
        return halves

    split = [(along_sublanes(base * s, q), along_sublanes(rise * s, q)) for q, s in ((0, depth_scale), (1, 1.0), (2, 1.0))]
    whole = along_lanes(base, 3), along_lanes(rise, 3)

    def level(q, scaled, k):
        if q == 3:
            return take(whole[0], k, 1) + take(whole[1], k, 1) * scaled
        low = k & (SUB - 1)
        parts = [jnp.where(scaled >= float(SUB), take(t[1], low, 0), take(t[0], low, 0)) for t in split[q]]
        return parts[0] + parts[1] * scaled

    def leave_copy(block, d):
        return pltpu.make_async_remote_copy(
            src_ref=leave.at[block], dst_ref=leave_in.at[x, block],
            send_sem=leave_send.at[d, block], recv_sem=leave_recv.at[x, block],
            device_id={"light": (x + d) % nx}, device_id_type=MESH,
        )

    def first(block):
        pltpu.make_async_copy(dens.at[block], dens.at[block], dens_sem.at[block]).wait()

        def rows(tile, sums):
            sums = list(sums)
            for row in range(SUB):
                for b in range(layers):
                    scaled = dens[block, b, tile, pl.ds(row, SUB, stride=SUB), :] * float(knots - 1)
                    k = scaled.astype(jnp.int32)
                    depth = level(0, scaled, k)
                    keep[block, tile * SUB + row, b] = jnp.exp2(depth)
                    cells[block, tile * SUB + row, b] = scaled
                    knot[block, tile * SUB + row, b] = k
                    sums[b] = sums[b] + depth
            return tuple(sums)

        zero = jnp.zeros((SUB, LANES), jnp.float32)
        sums = lax.fori_loop(0, tiles_a, rows, (zero,) * layers)
        for b in range(layers):
            leave[block, pl.ds(b * SUB, SUB)] = jnp.exp2(sums[b] * 2.0)
        if block == 0:
            pl.semaphore_wait(barrier, len(peers))
        for d in range(1, nx):

            @pl.when(x + d < nx)
            def _(d=d):
                leave_copy(block, d).start()

    wide = (SUB + 2) * LANES

    def light_up(block):
        fronts[...] = jnp.ones_like(fronts)
        before = jnp.maximum(block - 1, 0)
        behind = jnp.minimum(block + 1, blocks - 1)
        for stage in range(nx - 1):

            @pl.when(x > stage)
            def _(stage=stage):
                def gone_of(at, t):
                    return leave_in[stage, at, pl.ds(t, layers, stride=SUB), :]

                gone = [jnp.where(block > 0, gone_of(before, SUB - 1), 0.0)]
                gone += [gone_of(block, t) for t in range(SUB)]
                gone += [jnp.where(block < blocks - 1, gone_of(behind, 0), 0.0)]
                gone = jnp.concatenate(gone, axis=1)
                for drift in (-1, 0, 1):
                    value = fronts[drift + 1] * gone
                    sides = pltpu.roll(value, (drift - 1) % wide, 1) if drift != 1 else value
                    sides = sides + (pltpu.roll(value, (drift + 1) % wide, 1) if drift != -1 else value)
                    center = pltpu.roll(value, drift % wide, 1) if drift else value
                    fronts[drift + 1] = 0.25 * sides + 0.5 * center

        for k in range(3):
            tint = [0.0, 0.0, 0.0]
            for l in range(lights):
                for drift in (-1, 0, 1):
                    tint[drift + 1] = tint[drift + 1] + jnp.where(code_ref[l] == drift, tint_ref[l, k], 0.0)
            for t in range(SUB):
                cols = pl.ds((t + 1) * LANES, LANES)
                light[k, block, pl.ds(t, layers, stride=SUB), :] = (
                    fronts[0, :, cols] * tint[0] + fronts[1, :, cols] * tint[1] + fronts[2, :, cols] * tint[2]
                )

    def leaves_arrive(block):
        for stage in range(nx - 1):

            @pl.when(x > stage)
            def _(stage=stage):
                pltpu.make_async_copy(
                    leave_in.at[stage, block], leave_in.at[stage, block], leave_recv.at[stage, block]
                ).wait()

    pieces = blocks * ny
    quad = NZ // 2
    half = z // quad
    q = z % quad
    last = quad - 1
    up_base = half * quad
    down_base = quad - up_base
    own_base = (z + NZ - 2 - q // last) % NZ
    toward = 2 * (q // last) - 1
    own = q // last

    def core_copy(n):
        return pltpu.make_async_remote_copy(
            src_ref=part.at[n, 1 - core], dst_ref=core_in.at[n],
            send_sem=core_send.at[n], recv_sem=core_recv.at[n],
            device_id=at_view(y, z, 1 - core), device_id_type=MESH,
        )

    def up_copy(n):
        return pltpu.make_async_remote_copy(
            src_ref=part.at[n, core, pl.ds(up_base, quad)], dst_ref=up_in.at[n],
            send_sem=up_send.at[n], recv_sem=up_recv.at[n],
            device_id=at_view(y, (z + 1) % NZ, core), device_id_type=MESH,
        )

    def down_copy(n):
        return pltpu.make_async_remote_copy(
            src_ref=part.at[n, core, pl.ds(down_base, quad)], dst_ref=down_in.at[n],
            send_sem=down_send.at[n], recv_sem=down_recv.at[n],
            device_id=at_view(y, (z + NZ - 1) % NZ, core), device_id_type=MESH,
        )

    def cross_copy(n):
        return pltpu.make_async_remote_copy(
            src_ref=part.at[n, core, pl.ds((own_base + 2 * toward + NZ) % NZ, 2)], dst_ref=cross_in.at[n],
            send_sem=cross_send.at[n], recv_sem=cross_recv.at[n],
            device_id=at_view(y, (z + toward + NZ) % NZ, core), device_id_type=MESH,
        )

    buddy = z + 1 - 2 * (z % 2)

    def y_copy(n, to, source):
        return pltpu.make_async_remote_copy(
            src_ref=y_part.at[n, own], dst_ref=y_in.at[n // ny, source],
            send_sem=y_send.at[n], recv_sem=y_recv.at[n // ny, source],
            device_id=at_view(to, z, core), device_id_type=MESH,
        )

    def buddy_copy(n, to, source):
        return pltpu.make_async_remote_copy(
            src_ref=y_part.at[n, 1 - own], dst_ref=y_in.at[n // ny, source],
            send_sem=rest_send.at[n], recv_sem=y_recv.at[n // ny, source],
            device_id=at_view(to, buddy, core), device_id_type=MESH,
        )

    is_end = jnp.logical_or(q == 0, q == last)

    def ordered(later, mine, other):
        front = [jnp.where(later, o, m) for m, o in zip(mine, other)]
        back = [jnp.where(later, m, o) for m, o in zip(mine, other)]
        return over(front, back)

    def second(n):
        block, yy = n // ny, n % ny

        @pl.when(yy == 0)
        def _():
            shades[...] = jnp.ones_like(shades)

        def rows(i, shadow):
            shadow = list(shadow)
            tile = yy * 2 + i
            for row in range(SUB):
                clear = None
                total = [None] * 3
                for b in range(layers):
                    scaled = cells[block, tile * SUB + row, b]
                    k = knot[block, tile * SUB + row, b]
                    stays = keep[block, tile * SUB + row, b]
                    if clear is None:
                        weight = (1.0 - stays) * shadow[b]
                        clear = stays
                    else:
                        after = clear * stays
                        weight = (clear - after) * shadow[b]
                        clear = after
                    shadow[b] = shadow[b] * (stays * stays)
                    for c in range(3):
                        color = level(c + 1, scaled, k)
                        term = color * (weight * light[c, block, pl.ds(b * SUB, SUB), :])
                        total[c] = term if total[c] is None else total[c] + term
                slot = (i * (SUB // NCORE) + row // NCORE + NZ - 2) % NZ
                for c in range(3):
                    part[n, row % NCORE, slot, c] = total[c]
                part[n, row % NCORE, slot, 3] = clear
            return tuple(shadow)

        shadow = lax.fori_loop(0, 2, rows, tuple(shades[b] for b in range(layers)))
        for b in range(layers):
            shades[b] = shadow[b]

    def join(n, first, count, incoming, later):
        for i in range(count):
            mine = [part[n, core, first + i, k] for k in range(4)]
            joined = ordered(later, mine, [incoming[n, i, k] for k in range(4)])
            for k in range(4):
                part[n, core, first + i, k] = joined[k]

    def due(n):
        return jnp.logical_and(n >= 0, n < pieces)

    core_lag, hop_lag, cross_lag, y_lag = 1, 3, 6, 6
    steps = pieces + core_lag + last * hop_lag + cross_lag + y_lag

    ahead = blocks - 1
    for block in range(ahead):
        first(block)

    @pl.loop(0, steps)
    def _(step):
        @pl.when(step == 1)
        def _():
            for block in range(ahead, blocks):
                first(block)

        @pl.when(jnp.logical_and(step % ny == 0, step < pieces))
        def _():
            block = step // ny

            @pl.when(block == 0)
            def _():
                leaves_arrive(0)

            @pl.when(block < blocks - 1)
            def _():
                leaves_arrive(block + 1)

            light_up(block)

        @pl.when(step < pieces)
        def _():
            second(step)
            core_copy(step).start()

        at = step - core_lag

        @pl.when(due(at))
        def _():
            core_copy(at).wait_recv()
            join(at, 0, NZ, core_in, core == 1)

            @pl.when(q == 0)
            def _():
                up_copy(at).start()

            @pl.when(q == last)
            def _():
                down_copy(at).start()

        up_at = at - hop_lag * q

        @pl.when(jnp.logical_and(due(up_at), q > 0))
        def _():
            up_copy(up_at).wait_recv()
            join(up_at, up_base, quad, up_in, q > 0)

            @pl.when(q < last)
            def _():
                up_copy(up_at).start()

            @pl.when(q == last)
            def _():
                cross_copy(up_at).start()

        down_at = at - hop_lag * (last - q)

        @pl.when(jnp.logical_and(due(down_at), q < last))
        def _():
            down_copy(down_at).wait_recv()
            join(down_at, down_base, quad, down_in, q < 0)

            @pl.when(q > 0)
            def _():
                down_copy(down_at).start()

            @pl.when(q == 0)
            def _():
                cross_copy(down_at).start()

        cross_at = at - hop_lag * last - cross_lag

        @pl.when(jnp.logical_and(due(cross_at), is_end))
        def _():
            cross_copy(cross_at).wait_recv()
            to = cross_at % ny
            for i in range(2):
                mine = [part[cross_at, core, own_base + i, k] for k in range(4)]
                joined = ordered(half == 1, mine, [cross_in[cross_at, i, k] for k in range(4)])
                for k in range(4):
                    y_part[cross_at, i, k] = joined[k]

            @pl.when(to != y)
            def _():
                y_copy(cross_at, to, y).start()

            buddy_copy(cross_at, to, y).start()

        y_at = cross_at - y_lag

        @pl.when(jnp.logical_and(due(y_at), y_at % ny == y))
        def _():
            block = y_at // ny

            @pl.when(is_end)
            def _():
                for k in range(4):
                    y_in[block, y, k] = y_part[y_at, own, k]

            @pl.when(jnp.logical_not(is_end))
            def _():
                y_copy(y_at, y, y).wait_recv()

            for i in range(1, ny):
                source = (y + i) % ny
                y_copy(y_at, source, source).wait_recv()
            total = [y_in[block, 0, k] for k in range(4)]
            for j in range(1, ny):
                total = over(total, [y_in[block, j, k] for k in range(4)])
            for k in range(4):
                out_ref[k, pl.ds(block * SUB, SUB)] = total[k]

    for block in range(blocks):
        for d in range(1, nx):

            @pl.when(x + d < nx)
            def _(d=d, block=block):
                leave_copy(block, d).wait_send()

    @pl.loop(0, pieces)
    def _(n):
        core_copy(n).wait_send()

        @pl.when(q < last)
        def _():
            up_copy(n).wait_send()

        @pl.when(q > 0)
        def _():
            down_copy(n).wait_send()

        @pl.when(is_end)
        def _():
            cross_copy(n).wait_send()
            buddy_copy(n, n % ny, y).wait_send()

            @pl.when(n % ny != y)
            def _():
                y_copy(n, n % ny, y).wait_send()


def local(density, tables, table_index, light_code, light_tint):
    layers, slices, columns = density.shape
    nx, ny = lax.axis_size("light"), lax.axis_size("view") // (NZ * NCORE)
    table_count, _, knots = tables.shape
    tiles = columns // LANES
    blocks = tiles // SUB
    tiled = density.reshape(layers, slices // SUB, SUB, tiles, LANES).transpose(0, 1, 3, 2, 4)
    tiled = tiled.reshape(layers, slices // SUB, tiles * SUB, LANES)
    pieces = blocks * ny
    f32 = jnp.float32
    image = pl.pallas_call(
        functools.partial(kernel, nx, ny, layers, slices, columns, knots, table_count, light_code.shape[0]),
        out_shape=jax.ShapeDtypeStruct((4, tiles, LANES), f32),
        in_specs=[pl.BlockSpec(memory_space=pltpu.SMEM)] * 3
        + [pl.BlockSpec(memory_space=pltpu.VMEM), pl.BlockSpec(memory_space=pl.ANY)],
        out_specs=pl.BlockSpec(memory_space=pltpu.VMEM),
        scratch_shapes=[
            pltpu.VMEM((blocks, layers, slices // SUB, SUB * SUB, LANES), f32),
            pltpu.VMEM((blocks, slices, layers, SUB, LANES), f32),
            pltpu.VMEM((blocks, slices, layers, SUB, LANES), jnp.int32),
            pltpu.VMEM((blocks, slices, layers, SUB, LANES), f32),
            pltpu.VMEM((SUB, LANES), f32),
            pltpu.VMEM((blocks, layers * SUB, LANES), f32),
            pltpu.VMEM((nx, blocks, layers * SUB, LANES), f32),
            pltpu.VMEM((3, layers, (SUB + 2) * LANES), f32),
            pltpu.VMEM((3, blocks, layers * SUB, LANES), f32),
            pltpu.VMEM((layers, SUB, LANES), f32),
            pltpu.VMEM((pieces, NCORE, NZ, 4, SUB, LANES), f32),
            pltpu.VMEM((pieces, NZ, 4, SUB, LANES), f32),
            pltpu.VMEM((pieces, NZ // 2, 4, SUB, LANES), f32),
            pltpu.VMEM((pieces, NZ // 2, 4, SUB, LANES), f32),
            pltpu.VMEM((pieces, 2, 4, SUB, LANES), f32),
            pltpu.VMEM((pieces, 2, 4, SUB, LANES), f32),
            pltpu.VMEM((blocks, ny, 4, SUB, LANES), f32),
            pltpu.SemaphoreType.DMA((blocks,)),
            pltpu.SemaphoreType.DMA((nx, blocks)),
            pltpu.SemaphoreType.DMA((nx, blocks)),
        ]
        + [pltpu.SemaphoreType.DMA((pieces,))] * 9
        + [
            pltpu.SemaphoreType.DMA((blocks, ny)),
            pltpu.SemaphoreType.DMA((pieces,)),
        ],
        compiler_params=pltpu.CompilerParams(
            collective_id=0, has_side_effects=True, vmem_limit_bytes=60 * 1024 * 1024
        ),
    )(table_index, light_code, light_tint, tables, tiled)
    return image.reshape(4, 1, columns)


def solution(mesh):
    return jax.shard_map(
        local,
        mesh=mesh,
        in_specs=(P("view", "light", None), P(), P("light", "view"), P(), P()),
        out_specs=P(None, ("light", "view"), None),
        check_vma=False,
    )
```
